32 devices in a mesh: groups: 2 (over x), seq: 16 (over z, y, core).
Axes of the slice: x: 2, y: 2, z: 4, core: 2. Of those that a mesh axis runs over, the one named last changes fastest.
Arguments:
- latent: bfloat16 [32, 32768], P(('groups', 'seq')), parts along dimension 0, may hold values from -6 to 6
- text_embed: bfloat16 [4, 128, 3072], P('groups'), parts along dimension 0, may hold values from -6 to 6
- text_mask: int32 [4, 128], P('groups'), parts along dimension 0, may hold values from 0 to 1, as said below
- modulation: float32 [4, 5, 3072], P('groups'), parts along dimension 0, may hold values from -3 to 10
- w_in: bfloat16 [64, 3072], replicated, may hold values from -0.75 to 0.75
- w_qkv: bfloat16 [3072, 4608], P(None, 'seq'), may hold values from -0.109375 to 0.109375
- w_attn_out: bfloat16 [1536, 3072], P(None, 'seq'), may hold values from -0.15625 to 0.15625
- w_final: bfloat16 [3072, 64], replicated, may hold values from -0.109375 to 0.109375
Outputs:
- guided: float32 [32, 32768], P(('groups', 'seq')), parts along dimension 0
The draws below stay inside these ranges and needn't reach their ends.
There are 2 independent parts, one for each index of `groups`. The reference program is written for one: setup_inputs(seed, part) draws one part's arguments, and reference() takes and returns one part's arrays. A program takes and returns all parts, laid end to end along the dimension named above; an argument that names none is the same for every part. Nothing has to cross between parts.
Inputs may be any that keep to these rules, and one draw needn't show every extreme that they name: `text_mask`: each row is 1 on a leading run of 1 to 127 positions and 0 after it.
All inputs are finite; a program needn't handle non-finite values.
Results may differ from the reference program's by a relative error of at most 0.007.
The reference program's roundings to bfloat16 on the way count: a program that leaves them out, or rounds other values in their place, can miss the bound.
Values may be sent and summed in bfloat16 or wider, within the bound.
A program may use at most 128 MiB of HBM per device.

```python
import jax
import jax.numpy as jnp
from jax import lax

D = 3072
HDIM = 128
SHEADS = 6
THEADS = 6
CHAN = 64
POS = 512
TXT = 128
HEADS = 12
FRAMES = 16
HALF = 8


def draw_text_mask(key, part):
    lengths = jax.random.randint(jax.random.fold_in(key, 7), (2, 1), 1, TXT)
    places = jnp.arange(TXT, dtype=jnp.int32)[None, :]
    return (places < lengths).astype(jnp.int32)


def draw_modulation(key, part):
    base = jnp.clip(0.5 * jax.random.normal(jax.random.fold_in(key, 11), (2, 5, D), jnp.float32), -3.0, 3.0)
    return base


def block_levels(key, dims, split, smallest, top_value):
    def one(dim, shards_of):
        steps = jax.random.uniform(jax.random.fold_in(jax.random.fold_in(key, 6), dim), (shards_of,), jnp.float32, smallest / len(split), top_value / len(split))
        return jnp.repeat(jnp.exp(steps), dims[dim] // shards_of).reshape((-1,) + (1,) * (len(dims) - dim - 1))

    factor_of = one(*split[0])
    for cut in split[1:]:
        factor_of = factor_of * one(*cut)
    return factor_of


def scatter_about(own_key, extent, width, reach, pieces=(), held_as=jnp.bfloat16):
    entries = width * jax.random.normal(own_key, extent, jnp.float32)
    if pieces:
        entries = entries * block_levels(own_key, extent, pieces, -0.22, 0.18)
    return jnp.clip(entries, -reach, reach).astype(held_as)


def setup_inputs(seed: int = 0, part: int = 0) -> dict:
    key_list = jax.random.split(jax.random.key(seed), 9)
    part_keys = jax.random.split(jax.random.fold_in(key_list[8], part), 9)
    latent = scatter_about(part_keys[0], (FRAMES, POS * CHAN), 1.0, 6.0, ((0, 16),))
    text_embed = scatter_about(part_keys[1], (2, TXT, D), 1.0, 6.0)
    text_mask = draw_text_mask(jax.random.fold_in(jax.random.fold_in(key_list[8], part), 71), part)
    modulation = draw_modulation(jax.random.fold_in(jax.random.fold_in(key_list[8], part), 71), part)
    w_in = scatter_about(key_list[4], (CHAN, D), CHAN ** -0.5, 0.75)
    w_qkv = scatter_about(key_list[5], (D, 3 * HEADS * HDIM), D ** -0.5, 0.109375, ((1, 16),))
    w_attn_out = scatter_about(key_list[6], (HEADS * HDIM, D), (HEADS * HDIM) ** -0.5, 0.15625, ((1, 16),))
    w_final = scatter_about(key_list[7], (D, CHAN), D ** -0.5, 0.109375)
    return {"latent": latent, "text_embed": text_embed, "text_mask": text_mask, "modulation": modulation, "w_in": w_in, "w_qkv": w_qkv, "w_attn_out": w_attn_out, "w_final": w_final}


EPS = 1e-06
GUIDE = 5.0

def normalize(values):
    center = values - lax.optimization_barrier(jnp.mean(values, axis=-1, keepdims=True))
    spread = lax.optimization_barrier(jnp.mean(center * center, axis=-1, keepdims=True))
    return center * lax.rsqrt(spread + EPS)

def attend(query, keys, values, live):
    scores = jnp.einsum('qhe,khe->hqk', query.astype(jnp.float32), keys.astype(jnp.float32)) * HDIM ** (-0.5)
    scores = jnp.where(live[None, None, :], scores, -1e+30)
    top = lax.optimization_barrier(jnp.max(scores, axis=-1, keepdims=True))
    weights = jnp.exp(scores - top)
    total = lax.optimization_barrier(jnp.sum(weights, axis=-1, keepdims=True))
    probs = weights.astype(jnp.bfloat16)
    mixed = jnp.einsum('hqk,khe->qhe', probs.astype(jnp.float32), values.astype(jnp.float32))
    return (mixed / jnp.transpose(total, (1, 0, 2))).astype(jnp.bfloat16)

def temporal_mix(block):
    frames, span, heads = (block.shape[0], block.shape[1], block.shape[3])
    grid = block.reshape(2, frames // 2, span, 3, heads, HDIM).astype(jnp.float32)
    scores = jnp.einsum('afpne,agpne->apnfg', grid[:, :, :, 0], grid[:, :, :, 1]) * HDIM ** (-0.5)
    top = lax.optimization_barrier(jnp.max(scores, axis=-1, keepdims=True))
    weights = jnp.exp(scores - top)
    total = lax.optimization_barrier(jnp.sum(weights, axis=-1))
    probs = weights.astype(jnp.bfloat16)
    mixed = jnp.einsum('apnfg,agpne->afpne', probs.astype(jnp.float32), grid[:, :, :, 2])
    mixed = mixed / jnp.moveaxis(total, 3, 1)[..., None]
    return mixed.astype(jnp.bfloat16).reshape(frames, span, heads, HDIM)

def reference(latent, text_embed, text_mask, modulation, w_in, w_qkv, w_attn_out, w_final):
    halves = (jnp.arange(FRAMES) // HALF).astype(jnp.int32)

    def spatial(item):
        row, half = item
        start = jnp.dot(row.reshape(POS, CHAN), w_in, preferred_element_type=jnp.float32)
        mods = modulation[half]
        hidden = (normalize(start) * (1.0 + mods[1]) + mods[0]).astype(jnp.bfloat16)
        rows = jnp.concatenate([hidden, text_embed[half]], axis=0)
        projected = jnp.dot(rows, w_qkv, preferred_element_type=jnp.float32).astype(jnp.bfloat16)
        projected = projected.reshape(POS + TXT, 3, HEADS, HDIM)
        live = jnp.concatenate([jnp.ones((POS,), bool), text_mask[half] > 0])
        spatial_out = attend(projected[:POS, 0, :SHEADS], projected[:, 1, :SHEADS], projected[:, 2, :SHEADS], live)
        return (start, spatial_out, projected[:POS, :, SHEADS:])
    starts, spatial_outs, temporal_in = lax.map(spatial, (latent, halves))
    temporal_outs = temporal_mix(temporal_in)

    def finish(item):
        start, spatial_out, temporal_out, half = item
        mods = modulation[half]
        joined = jnp.concatenate([spatial_out.reshape(POS, SHEADS * HDIM), temporal_out.reshape(POS, THEADS * HDIM)], axis=1)
        block = start + mods[2] * jnp.dot(joined, w_attn_out, preferred_element_type=jnp.float32)
        final = (normalize(block) * (1.0 + mods[4]) + mods[3]).astype(jnp.bfloat16)
        return jnp.dot(final, w_final, preferred_element_type=jnp.float32).astype(jnp.bfloat16)
    preds = lax.map(finish, (starts, spatial_outs, temporal_outs, halves)).astype(jnp.float32)
    cond_pred = preds[:HALF]
    uncond_pred = preds[HALF:]
    mixed = uncond_pred + GUIDE * (cond_pred - uncond_pred)
    return jnp.concatenate([mixed, mixed], axis=0).reshape(FRAMES, POS * CHAN)
```

```python
import functools

import jax
import jax.numpy as jnp
from jax import lax
from jax.experimental import pallas as pl
from jax.experimental.pallas import tpu as pltpu
from jax.sharding import PartitionSpec as P

HDIM = 128
SHEADS = 6
THEADS = 6
CHAN = 64
HEADS = 12
ROLES = 4
SROLES = 2

EPS = 1e-06
GUIDE = 5.0
NT = (((1,), (1,)), ((), ()))


def dot_nt(a, b):
    return lax.dot_general(a, b, NT, preferred_element_type=jnp.float32)


def normalize(values):
    center = values - jnp.mean(values, axis=-1, keepdims=True)
    spread = jnp.mean(center * center, axis=-1, keepdims=True)
    return center * lax.rsqrt(spread + EPS)


def block_kernel(
    count, gran, lat, text, mask, mods, w_in, wq, wo, wf, out,
    latbuf, wbuf, hbuf, tbuf, pbuf, obuf, wob, jbuf, blk, acc, predb,
    lat_send, lat_recv, w_send, w_xsend, w_tsend, w_recv, wo_send, wo_xsend, wo_tsend, wo_recv,
    j_send, j_recv, p_send, p_recv, loc,
):
    positions = lat.shape[0]
    depth = w_in.shape[1]
    n2 = count // 2
    chips = n2 // 2
    team, me = lax.axis_index("groups"), lax.axis_index("seq")
    plane = lax.rem(team, 2)
    half = lax.div(me, n2)
    local = lax.rem(me, n2)
    core = lax.rem(me, 2)
    chip = lax.div(local, 2)
    role = lax.rem(chip, ROLES)
    members = n2 // ROLES
    pairs = members // 2
    spot = lax.div(chip, ROLES) * 2 + core
    span = positions // members
    rows = ROLES * positions
    width = wbuf.shape[1]
    offs = width // gran
    per_part = ROLES * offs
    mine = wq.shape[0] // gran
    is_spatial = role < SROLES

    twin = {"seq": me + 1 - 2 * core}
    across = {"groups": team + 1 - 2 * plane}

    def device(side, which, at):
        return side * n2 + (lax.div(at, 2) * ROLES + which) * 2 + lax.rem(at, 2)

    def remote(src, dst, send, recv, peer):
        return pltpu.make_async_remote_copy(
            src_ref=src, dst_ref=dst, send_sem=send, recv_sem=recv,
            device_id=peer, device_id_type=pl.DeviceIdType.MESH,
        )

    finish = []

    def go(src, dst, send, recv, peer):
        remote(src, dst, send, recv, peer).start()
        finish.append(lambda: remote(src, dst, send, recv, peer).wait_send())

    def push(src, dst, send, recv, to):
        def far():
            return remote(src, dst, send, recv, {"seq": to})

        @pl.when(to == me)
        def _():
            pltpu.make_async_copy(src, dst, recv).start()

        @pl.when(to != me)
        def _():
            far().start()

        def end():
            @pl.when(to != me)
            def _():
                far().wait_send()

        finish.append(end)

    def arrived(view, sem):
        pltpu.make_async_copy(view, view, sem).wait()

    def aligned(value, unit):
        return pl.multiple_of(value, unit)

    barrier = pltpu.get_barrier_semaphore()

    def greet(step, carry):
        peer = lax.rem(me + step, count)
        pl.semaphore_signal(barrier, inc=1, device_id={"seq": peer}, device_id_type=pl.DeviceIdType.MESH)
        return carry

    pl.semaphore_signal(barrier, inc=1, device_id=across, device_id_type=pl.DeviceIdType.MESH)
    lax.fori_loop(1, count, greet, 0)

    shard = wo.shape[0]
    unit = shard // 3
    own_wo = pltpu.make_async_copy(wo, wob.at[pl.ds(aligned(me * shard, shard), shard)], loc.at[0])
    own_text = pltpu.make_async_copy(text.at[half], tbuf, loc.at[1])
    own_wo.start()
    own_text.start()
    pl.semaphore_wait(barrier, count)

    for which in range(SROLES):
        to = device(half, which, lax.div(local, ROLES))
        slot = lax.rem(local, ROLES)
        push(
            lat, latbuf.at[pl.ds(aligned(slot * positions, positions), positions)],
            lat_send.at[which], lat_recv.at[slot], to,
        )
    for which in range(SROLES, ROLES):
        for at in range(members):
            push(
                lat.at[pl.ds(at * span, span)], latbuf.at[pl.ds(aligned(local * span, span), span)],
                lat_send.at[SROLES + (which - SROLES) * members + at], lat_recv.at[local],
                device(half, which, jnp.int32(at)),
            )

    def slot_view(part, off):
        return wbuf.at[part, pl.ds(aligned(off * gran, gran), gran)]

    def w_sem(part, off):
        return part * offs + off

    for far in (1, 0):
        for k in range(mine):
            number = me * mine + k
            part = lax.div(number, per_part)
            which = lax.div(lax.rem(number, per_part), offs)
            off = lax.rem(number, offs)
            side = half + far * (1 - 2 * half)
            for pair in range(pairs):
                to = side * n2 + (pair * ROLES + which) * 2 + lax.rem(off, 2)

                def send(k=k, part=part, off=off, to=to, far=far, pair=pair):
                    return (
                        wq.at[pl.ds(k * gran, gran)], slot_view(part, off),
                        w_send.at[k, far, pair], w_recv.at[w_sem(part, off)],
                    )

                turn = lax.rem(lax.div(off, 2), 2) == plane

                @pl.when(jnp.logical_and(turn, to == me))
                def _(send=send):
                    src, dst, _, recv = send()
                    pltpu.make_async_copy(src, dst, recv).start()

                @pl.when(jnp.logical_and(turn, to != me))
                def _(send=send, to=to):
                    remote(*send(), {"seq": to}).start()

                def end(send=send, to=to, turn=turn):
                    @pl.when(jnp.logical_and(turn, to != me))
                    def _():
                        remote(*send(), {"seq": to}).wait_send()

                finish.append(end)

    def wo_direct(owner):
        return pl.ds(aligned(owner * shard + plane * unit, unit), 2 * unit)

    def wo_cross(owner, side):
        return pl.ds(aligned(owner * shard + side * 2 * unit, unit), unit)

    mirror = me + n2 * (1 - 2 * half)
    own_direct = wo.at[pl.ds(aligned(plane * unit, unit), 2 * unit)]

    def in_half(step):
        return half * n2 + lax.rem(chip + step, chips) * 2 + core

    def in_other(step):
        return (1 - half) * n2 + lax.rem(chip + step, chips) * 2 + core

    go(own_direct, wob.at[wo_direct(me)], wo_send.at[0, 0], wo_recv.at[me, 0], {"seq": mirror})
    for step in range(1, chips):
        go(
            own_direct, wob.at[wo_direct(me)], wo_send.at[0, step], wo_recv.at[me, 0],
            {"seq": in_half(step)},
        )
    own_rows = wob.at[pl.ds(aligned(me * shard, shard), shard)]
    go(wo, own_rows, wo_tsend.at[0, 0], wo_recv.at[me, 0], twin)

    def wo_spread(owner, number):
        go(
            wob.at[wo_cross(owner, plane)], wob.at[wo_cross(owner, plane)],
            wo_xsend.at[number], wo_recv.at[owner, 1], across,
        )
        go(
            wob.at[wo_direct(owner)], wob.at[wo_direct(owner)],
            wo_tsend.at[1, number], wo_recv.at[owner, 0], twin,
        )

    def wo_take(owner, number):
        arrived(wob.at[wo_direct(owner)], wo_recv.at[owner, 0])
        wo_spread(owner, number)

    def wo_mirror():
        arrived(wob.at[wo_direct(mirror)], wo_recv.at[mirror, 0])
        for step in range(1, chips):
            go(
                wob.at[wo_direct(mirror)], wob.at[wo_direct(mirror)], wo_send.at[1, step],
                wo_recv.at[mirror, 0], {"seq": in_half(step)},
            )
        wo_spread(mirror, 0)

    def wo_others():
        return [(in_half(step), step) for step in range(1, chips)] + [
            (in_other(step), chips + step) for step in range(1, chips)
        ]

    def wo_cross_take():
        for owner, number in [(mirror, 0)] + wo_others():
            arrived(wob.at[wo_cross(owner, 1 - plane)], wo_recv.at[owner, 1])
            go(
                wob.at[wo_cross(owner, 1 - plane)], wob.at[wo_cross(owner, 1 - plane)],
                wo_tsend.at[2, number], wo_recv.at[owner, 1], twin,
            )

    def wo_wait():
        own_wo.wait()
        other = 1 - 2 * core
        arrived(wob.at[pl.ds(aligned((me + other) * shard, shard), shard)], wo_recv.at[me + other, 0])
        for owner, _ in [(mirror, 0)] + wo_others():
            arrived(wob.at[wo_direct(owner + other)], wo_recv.at[owner + other, 0])
            arrived(wob.at[wo_cross(owner + other, 1 - plane)], wo_recv.at[owner + other, 1])

    def mod(which):
        return jnp.where(half == 0, mods[which, 0:1, :], mods[which, 1:2, :])

    quarter = positions // 4

    def start_step(step, carry):
        at = pl.ds(aligned(step * quarter, quarter), quarter)
        blk[at, :] = jnp.dot(lat[at, :], w_in[...], preferred_element_type=jnp.float32)
        return carry

    lax.fori_loop(0, 4, start_step, 0)

    @pl.when(is_spatial)
    def _():
        for slot in range(ROLES):
            arrived(latbuf.at[pl.ds(slot * positions, positions)], lat_recv.at[slot])

    @pl.when(jnp.logical_not(is_spatial))
    def _():
        for frame in range(n2):
            arrived(latbuf.at[pl.ds(frame * span, span)], lat_recv.at[frame])

    tall = 128

    def hidden_step(step, carry):
        at = pl.ds(aligned(step * tall, tall), tall)
        begun = jnp.dot(latbuf[at, :], w_in[...], preferred_element_type=jnp.float32)
        hbuf[at, :] = (normalize(begun) * (1.0 + mod(1)) + mod(0)).astype(jnp.bfloat16)
        return carry

    lax.fori_loop(0, rows // tall, hidden_step, 0)
    own_text.wait()

    def order(step):
        return step + half * (2 - 2 * step)

    def first_take(step):
        part = order(step)
        for e in range(offs // 4):
            off = core + 2 * plane + 4 * e
            view, number = slot_view(part, off), w_sem(part, off)
            arrived(view, w_recv.at[number])
            go(view, view, w_xsend.at[number], w_recv.at[number], across)
            go(view, view, w_tsend.at[number], w_recv.at[number], twin)

    def second_take(step):
        part = order(step)
        for e in range(offs // 4):
            off = core + 2 * (1 - plane) + 4 * e
            view, number = slot_view(part, off), w_sem(part, off)
            arrived(view, w_recv.at[number])
            go(view, view, w_tsend.at[number], w_recv.at[number], twin)

    def third_take(step):
        part = order(step)
        for e in range(offs // 4):
            for side in range(2):
                off = 1 - core + 2 * side + 4 * e
                arrived(slot_view(part, off), w_recv.at[w_sem(part, off)])

    def project(step):
        part = order(step)

        def body(turn, carry):
            at = pl.ds(aligned(turn * positions, positions), positions)
            pbuf[part, at, :] = dot_nt(hbuf[at, :], wbuf[part]).astype(jnp.bfloat16)
            return carry

        lax.fori_loop(0, ROLES, body, 0)

        @pl.when(jnp.logical_and(is_spatial, part > 0))
        def _():
            pbuf[part, pl.ds(rows, tbuf.shape[0]), :] = dot_nt(tbuf[...], wbuf[part]).astype(jnp.bfloat16)

    first_take(0)
    first_take(1)
    second_take(0)
    third_take(0)
    project(0)
    first_take(2)
    second_take(1)
    third_take(1)
    wo_mirror()
    project(1)
    second_take(2)
    third_take(2)
    for owner, number in wo_others()[: chips - 1]:
        wo_take(owner, number)
    project(2)
    for owner, number in wo_others()[chips - 1 :]:
        wo_take(owner, number)

    scale = HDIM ** (-0.5)
    heads = width // HDIM
    words = tbuf.shape[0]
    lanes = pl.ds(aligned(role * width, width), width)

    def out_copy(src, dst, send, recv, to):
        return (src, dst, send, recv), to

    def spatial_send(frame):
        to = half * n2 + spot * ROLES + frame
        src = obuf.at[pl.ds(aligned(frame * positions, positions), positions)]
        return (src, jbuf.at[:, lanes], j_send.at[frame], j_recv.at[role]), to

    def temporal_send(frame):
        to = half * n2 + frame
        src = obuf.at[pl.ds(aligned(frame * span, span), span)]
        dst = jbuf.at[pl.ds(aligned(spot * span, span), span), lanes]
        recv = j_recv.at[SROLES + (role - SROLES) * members + spot]
        return (src, dst, j_send.at[frame], recv), to

    def dispatch(refs, to):
        src, dst, send, recv = refs

        @pl.when(to == me)
        def _():
            pltpu.make_async_copy(src, dst, recv).start()

        @pl.when(to != me)
        def _():
            remote(src, dst, send, recv, {"seq": to}).start()

    def drain(refs, to):
        @pl.when(to != me)
        def _():
            remote(*refs, {"seq": to}).wait_send()

    @pl.when(is_spatial)
    def _():
        live = jnp.where(half == 0, mask[0:1, :], mask[1:2, :]) > 0
        tallq = positions // 2

        def frame_step(frame, carry):
            base = frame * positions
            at = pl.ds(aligned(base, positions), positions)
            for head in range(heads):
                cols = pl.ds(head * HDIM, HDIM)
                keys, vals = pbuf[1, at, cols], pbuf[2, at, cols]
                tkeys, tvals = pbuf[1, pl.ds(rows, words), cols], pbuf[2, pl.ds(rows, words), cols]
                for piece in range(2):
                    here = pl.ds(aligned(base + piece * tallq, tallq), tallq)
                    query = pbuf[0, here, cols]
                    near = dot_nt(query, keys) * scale
                    side = jnp.where(live, dot_nt(query, tkeys) * scale, -1e30)
                    top = jnp.maximum(
                        jnp.max(near, axis=-1, keepdims=True), jnp.max(side, axis=-1, keepdims=True)
                    )
                    near = jnp.exp(near - top)
                    side = jnp.exp(side - top)
                    total = jnp.sum(near, axis=-1, keepdims=True) + jnp.sum(side, axis=-1, keepdims=True)
                    mixed = jnp.dot(
                        near.astype(jnp.bfloat16), vals, preferred_element_type=jnp.float32
                    ) + jnp.dot(side.astype(jnp.bfloat16), tvals, preferred_element_type=jnp.float32)
                    obuf[here, cols] = (mixed / total).astype(jnp.bfloat16)
            dispatch(*spatial_send(frame))
            return carry

        lax.fori_loop(0, ROLES, frame_step, 0)

    @pl.when(jnp.logical_not(is_spatial))
    def _():
        few = 256 // n2
        size = few * n2
        row_at = lax.rem(lax.broadcasted_iota(jnp.int32, (size, size), 0), few)
        col_at = lax.rem(lax.broadcasted_iota(jnp.int32, (size, size), 1), few)
        same = row_at == col_at

        def place_step(place, carry):
            def at(frame):
                return pl.ds(aligned(frame * span + place * few, few), few)

            for head in range(heads):
                cols = pl.ds(head * HDIM, HDIM)
                query, keys, vals = (
                    jnp.concatenate([pbuf[part, at(frame), cols] for frame in range(n2)], axis=0)
                    for part in range(3)
                )
                scores = jnp.where(same, dot_nt(query, keys) * scale, -1e30)
                weights = jnp.exp(scores - jnp.max(scores, axis=-1, keepdims=True))
                total = jnp.sum(weights, axis=-1, keepdims=True)
                mixed = jnp.dot(weights.astype(jnp.bfloat16), vals, preferred_element_type=jnp.float32)
                mixed = (mixed / total).astype(jnp.bfloat16)
                for frame in range(n2):
                    obuf[at(frame), cols] = mixed[frame * few : (frame + 1) * few]
            return carry

        lax.fori_loop(0, span // few, place_step, 0)

        def send_step(frame, carry):
            dispatch(*temporal_send(frame))
            return carry

        lax.fori_loop(0, n2, send_step, 0)

    wo_cross_take()
    wo_wait()
    for which in range(SROLES):
        arrived(jbuf.at[:, pl.ds(which * width, width)], j_recv.at[which])
    for which in range(SROLES, ROLES):
        for at in range(members):
            arrived(
                jbuf.at[pl.ds(at * span, span), pl.ds(which * width, width)],
                j_recv.at[SROLES + (which - SROLES) * members + at],
            )

    acc[...] = jnp.zeros_like(acc)
    strip = 512

    def mix_step(step, carry):
        cols = pl.ds(aligned(step * strip, strip), strip)
        gate = jnp.where(half == 0, mods[2, 0:1, cols], mods[2, 1:2, cols])
        value = blk[:, cols] + gate * dot_nt(jbuf[...], wob[cols, :])
        blk[:, cols] = value
        part = value[:, :128]
        for piece in range(1, strip // 128):
            part = part + value[:, piece * 128 : (piece + 1) * 128]
        acc[...] += part
        return carry

    lax.fori_loop(0, depth // strip, mix_step, 0)

    def swap(step):
        at = pl.ds(aligned(step * quarter, quarter), quarter)
        return remote(
            predb.at[0, at], predb.at[1, at], p_send.at[step], p_recv.at[step], {"seq": mirror}
        )

    def last_step(step, carry):
        at = pl.ds(aligned(step * quarter, quarter), quarter)
        mean = jnp.sum(acc[at, :], axis=-1, keepdims=True) / depth
        center = blk[at, :] - mean
        spread = jnp.mean(center * center, axis=-1, keepdims=True)
        final = center * lax.rsqrt(spread + EPS) * (1.0 + mod(4)) + mod(3)
        predb[0, at, :] = dot_nt(final.astype(jnp.bfloat16), wf[...]).astype(jnp.bfloat16)
        swap(step).start()
        return carry

    lax.fori_loop(0, 4, last_step, 0)

    def guide_step(step, carry):
        at = pl.ds(aligned(step * quarter, quarter), quarter)
        swap(step).wait_recv()
        own = predb[0, at, :].astype(jnp.float32)
        other = predb[1, at, :].astype(jnp.float32)
        cond = jnp.where(half == 0, own, other)
        uncond = jnp.where(half == 0, other, own)
        out[at, :] = uncond + GUIDE * (cond - uncond)
        return carry

    lax.fori_loop(0, 4, guide_step, 0)

    def swap_end(step, carry):
        swap(step).wait_send()
        return carry

    lax.fori_loop(0, 4, swap_end, 0)

    @pl.when(is_spatial)
    def _():
        def end(frame, carry):
            drain(*spatial_send(frame))
            return carry

        lax.fori_loop(0, ROLES, end, 0)

    @pl.when(jnp.logical_not(is_spatial))
    def _():
        def end(frame, carry):
            drain(*temporal_send(frame))
            return carry

        lax.fori_loop(0, n2, end, 0)

    for end in finish:
        end()


def per_device(latent, text_embed, text_mask, modulation, w_in, w_qkv, w_attn_out, w_final):
    count = lax.axis_size("seq")
    positions = latent.shape[1] // CHAN
    depth = w_in.shape[1]
    n2 = count // 2
    members = n2 // ROLES
    width = HEADS * HDIM // ROLES
    cols = w_qkv.shape[1]
    gran = next(g for g in range(min(cols, width), 0, -16) if cols % g == 0 and width % (4 * g) == 0)
    offs, mine = width // gran, cols // gran
    chips = n2 // 2
    rows = ROLES * positions
    words = text_embed.shape[1]
    bf16, f32 = jnp.bfloat16, jnp.float32
    vmem, anywhere = pl.BlockSpec(memory_space=pltpu.VMEM), pl.BlockSpec(memory_space=pl.ANY)
    sem = pltpu.SemaphoreType.DMA
    guided = pl.pallas_call(
        functools.partial(block_kernel, count, gran),
        out_shape=jax.ShapeDtypeStruct((positions, CHAN), f32),
        in_specs=[vmem, anywhere, vmem, vmem, vmem, anywhere, anywhere, vmem],
        out_specs=vmem,
        scratch_shapes=[
            pltpu.VMEM((rows, CHAN), bf16),
            pltpu.VMEM((3, width, depth), bf16),
            pltpu.VMEM((rows, depth), bf16),
            pltpu.VMEM((words, depth), bf16),
            pltpu.VMEM((3, rows + words, width), bf16),
            pltpu.VMEM((rows, width), bf16),
            pltpu.VMEM((depth, HEADS * HDIM), bf16),
            pltpu.VMEM((positions, HEADS * HDIM), bf16),
            pltpu.VMEM((positions, depth), f32),
            pltpu.VMEM((positions, 128), f32),
            pltpu.VMEM((2, positions, CHAN), bf16),
            sem((SROLES + (ROLES - SROLES) * members,)),
            sem((max(n2, ROLES),)),
            sem((mine, 2, members // 2)),
            sem((3 * offs,)),
            sem((3 * offs,)),
            sem((3 * offs,)),
            sem((2, chips)),
            sem((2 * chips,)),
            sem((3, 2 * chips)),
            sem((count, 2)),
            sem((max(n2, ROLES),)),
            sem((SROLES + (ROLES - SROLES) * members,)),
            sem((4,)),
            sem((4,)),
            sem((2,)),
        ],
        compiler_params=pltpu.CompilerParams(
            collective_id=0, has_side_effects=True, vmem_limit_bytes=64000 * 1024
        ),
        name="block",
    )(
        latent.reshape(positions, CHAN), text_embed, text_mask, jnp.transpose(modulation, (1, 0, 2)),
        w_in, w_qkv.T, w_attn_out.T, w_final.T,
    )
    return guided.reshape(1, positions * CHAN)


def solution(mesh):
    in_specs = (
        P(("groups", "seq"), None),
        P("groups", None, None),
        P("groups", None),
        P("groups", None, None),
        P(),
        P(None, "seq"),
        P(None, "seq"),
        P(),
    )
    out_specs = P(("groups", "seq"), None)
    return jax.shard_map(
        per_device, mesh=mesh, in_specs=in_specs, out_specs=out_specs, check_vma=False
    )
```

```python
import functools

import jax
import jax.numpy as jnp
from jax import lax
from jax.experimental import pallas as pl
from jax.experimental.pallas import tpu as pltpu
from jax.sharding import PartitionSpec as P

HDIM = 128
SHEADS = 6
THEADS = 6
CHAN = 64
HEADS = 12
ROLES = 4
SROLES = 2
ROLE_OF = ((0, 2, 3, 1), (2, 0, 1, 3))

EPS = 1e-06
GUIDE = 5.0
NT = (((1,), (1,)), ((), ()))


def pick(table, *at):
    if not at:
        return jnp.int32(table)
    picked = pick(table[0], *at[1:])
    for number in range(1, len(table)):
        picked = jnp.where(at[0] == number, pick(table[number], *at[1:]), picked)
    return picked


def dot_nt(a, b):
    return lax.dot_general(a, b, NT, preferred_element_type=jnp.float32)


def normalize(values):
    center = values - jnp.mean(values, axis=-1, keepdims=True)
    spread = jnp.mean(center * center, axis=-1, keepdims=True)
    return center * lax.rsqrt(spread + EPS)


def block_kernel(
    count, gran, lat, text, mask, mods, w_in, wq, wo, wf, out,
    latbuf, w_two, wf_two, wbuf, hbuf, tbuf, pbuf, obuf, wob, jbuf, blk, acc, predb,
    lat_send, lat_recv, w_send, w_xsend, w_tsend, w_recv, wo_send, wo_xsend, wo_tsend, wo_recv,
    j_send, j_recv, p_send, p_recv, loc,
):
    packed = lat.shape[0]
    positions = 2 * packed
    depth = w_in.shape[1]
    n2 = count // 2
    chips = n2 // 2
    team, me = lax.axis_index("groups"), lax.axis_index("seq")
    plane = lax.rem(team, 2)
    half = lax.div(me, n2)
    local = lax.rem(me, n2)
    core = lax.rem(me, 2)
    chip = lax.div(local, 2)
    role = pick(ROLE_OF, half, lax.rem(chip, ROLES))
    seat_of = [[row.index(which) for which in range(ROLES)] for row in ROLE_OF]
    members = n2 // ROLES
    pairs = members // 2
    spot = lax.div(chip, ROLES) * 2 + core
    span = positions // members
    rows = ROLES * positions
    width = wbuf.shape[1]
    heads = width // HDIM
    offs = HDIM // gran
    mine = wq.shape[0] // gran
    is_spatial = role < SROLES

    twin = {"seq": me + 1 - 2 * core}
    across = {"groups": team + 1 - 2 * plane}

    def device(side, which, at):
        return side * n2 + (lax.div(at, 2) * ROLES + pick(seat_of, side, which)) * 2 + lax.rem(at, 2)

    def remote(src, dst, send, recv, peer):
        return pltpu.make_async_remote_copy(
            src_ref=src, dst_ref=dst, send_sem=send, recv_sem=recv,
            device_id=peer, device_id_type=pl.DeviceIdType.MESH,
        )

    finish = []

    def go(src, dst, send, recv, peer):
        remote(src, dst, send, recv, peer).start()
        finish.append(lambda: remote(src, dst, send, recv, peer).wait_send())

    def push(src, dst, send, recv, to):
        def far():
            return remote(src, dst, send, recv, {"seq": to})

        @pl.when(to == me)
        def _():
            pltpu.make_async_copy(src, dst, recv).start()

        @pl.when(to != me)
        def _():
            far().start()

        def end():
            @pl.when(to != me)
            def _():
                far().wait_send()

        finish.append(end)

    def arrived(view, sem):
        pltpu.make_async_copy(view, view, sem).wait()

    def aligned(value, unit):
        return pl.multiple_of(value, unit)

    barrier = pltpu.get_barrier_semaphore()

    def greet(step, carry):
        peer = lax.rem(me + step, count)
        pl.semaphore_signal(barrier, inc=1, device_id={"seq": peer}, device_id_type=pl.DeviceIdType.MESH)
        return carry

    pl.semaphore_signal(barrier, inc=1, device_id=across, device_id_type=pl.DeviceIdType.MESH)
    lax.fori_loop(1, count, greet, 0)

    shard = wo.shape[0]
    unit = shard // (2 * heads)
    own_wo = pltpu.make_async_copy(wo, wob.at[pl.ds(aligned(me * shard, shard), shard)], loc.at[0])
    own_text = pltpu.make_async_copy(text.at[half], tbuf, loc.at[1])
    own_wo.start()
    own_text.start()
    chan = w_in.shape[0]
    none = jnp.zeros((chan, depth), jnp.bfloat16)
    for odd in range(2):
        for two, one in ((w_two, w_in), (wf_two, wf)):
            two[odd, pl.ds(odd * chan, chan), :] = one[...]
            two[odd, pl.ds((1 - odd) * chan, chan), :] = none
    pl.semaphore_wait(barrier, count)

    for which in range(SROLES):
        to = device(half, which, lax.div(local, ROLES))
        slot = lax.rem(local, ROLES)
        push(
            lat, latbuf.at[pl.ds(aligned(slot * packed, packed), packed)],
            lat_send.at[which], lat_recv.at[slot], to,
        )
    for which in range(SROLES, ROLES):
        for at in range(members):
            push(
                lat.at[pl.ds(at * span % packed, span)], latbuf.at[pl.ds(aligned(local * span, span), span)],
                lat_send.at[SROLES + (which - SROLES) * members + at], lat_recv.at[local],
                device(half, which, jnp.int32(at)),
            )

    def slot_view(head, part, off):
        return wbuf.at[head, pl.ds(aligned(part * HDIM + off * gran, gran), gran)]

    def slot_sem(head, part, off):
        return (head * 3 + part) * offs + off

    def crosses(head, part, off):
        column = (part * HEADS + role * heads + head) * HDIM + off * gran
        return lax.div(lax.div(column, wq.shape[0]), n2) != half

    def owner_loop(begin, head_first, head_last):
        def visit(turn, carry):
            wanted, k = lax.div(turn, mine), lax.rem(turn, mine)
            number = me * mine + k
            off = lax.rem(number, offs)
            whole = lax.div(number, offs)
            part, head_at = lax.div(whole, HEADS), lax.rem(whole, HEADS)
            which, head = lax.div(head_at, heads), lax.rem(head_at, heads)
            src = wq.at[pl.ds(aligned(k * gran, gran), gran)]
            dst, recv = slot_view(head, part, off), w_recv.at[slot_sem(head, part, off)]
            turned = lax.rem(lax.div(off, 2), 2) == plane
            for far in (1, 0):
                side = half + far * (1 - 2 * half)
                for pair in range(pairs):
                    to = device(side, which, pair * 2 + lax.rem(off, 2))
                    use = head == wanted
                    if far:
                        use = jnp.logical_and(use, turned)

                    @pl.when(jnp.logical_and(use, to != me))
                    def _(to=to, far=far, pair=pair):
                        copy = remote(src, dst, w_send.at[k, far, pair], recv, {"seq": to})
                        copy.start() if begin else copy.wait_send()

                    if begin and not far:

                        @pl.when(jnp.logical_and(use, to == me))
                        def _():
                            pltpu.make_async_copy(src, dst, recv).start()

            return carry

        lax.fori_loop(head_first * mine, head_last * mine, visit, 0)

    finish.append(lambda: owner_loop(False, 0, heads))

    def wo_view(owner, side, piece):
        if piece == heads - 1:
            return wob.at[pl.ds(aligned(owner * shard + 2 * piece * unit, unit), 2 * unit)]
        return wob.at[pl.ds(aligned(owner * shard + (2 * piece + side) * unit, unit), unit)]

    mirror = me + n2 * (1 - 2 * half)

    def in_half(step):
        return half * n2 + lax.rem(chip + step, chips) * 2 + core

    def in_other(step):
        return (1 - half) * n2 + lax.rem(chip + step, chips) * 2 + core

    def wo_own_sends(piece):
        if piece == heads - 1:
            src = wo.at[pl.ds(2 * piece * unit, 2 * unit)]
        else:
            src = wo.at[pl.ds(aligned((2 * piece + plane) * unit, unit), unit)]
        dst, recv = wo_view(me, plane, piece), wo_recv.at[piece, me, 0]
        go(src, dst, wo_send.at[piece, 0, 0], recv, {"seq": mirror})
        for step in range(1, chips):
            go(src, dst, wo_send.at[piece, 0, step], recv, {"seq": in_half(step)})

    def wo_spread(owner, number, piece):
        view = wo_view(owner, plane, piece)
        if piece < heads - 1:
            go(view, view, wo_xsend.at[piece, number], wo_recv.at[piece, owner, 1], across)
        go(view, view, wo_tsend.at[piece, 0, number], wo_recv.at[piece, owner, 0], twin)

    def wo_take(owner, number, piece):
        arrived(wo_view(owner, plane, piece), wo_recv.at[piece, owner, 0])
        wo_spread(owner, number, piece)

    others = [(in_half(step), step) for step in range(1, chips)]
    far_others = [(in_other(step), chips + step) for step in range(1, chips)]

    def wo_near_take(piece):
        for owner, number in others:
            wo_take(owner, number, piece)

    def wo_mirror(piece):
        view = wo_view(mirror, plane, piece)
        arrived(view, wo_recv.at[piece, mirror, 0])
        for step in range(1, chips):
            go(
                view, view, wo_send.at[piece, 1, step], wo_recv.at[piece, mirror, 0],
                {"seq": in_half(step)},
            )
        wo_spread(mirror, 0, piece)

    def wo_far_take(piece):
        for owner, number in far_others:
            wo_take(owner, number, piece)

    def wo_cross_take(piece, owners):
        for owner, number in owners:
            view = wo_view(owner, 1 - plane, piece)
            arrived(view, wo_recv.at[piece, owner, 1])
            go(view, view, wo_tsend.at[piece, 1, number], wo_recv.at[piece, owner, 1], twin)

    def wo_wait(owners):
        for piece in range(heads):
            for owner, _ in owners:
                owner = owner + 1 - 2 * core
                arrived(wo_view(owner, plane, piece), wo_recv.at[piece, owner, 0])
                if piece < heads - 1:
                    arrived(wo_view(owner, 1 - plane, piece), wo_recv.at[piece, owner, 1])

    def wo_own_wait():
        own_wo.wait()
        other = me + 1 - 2 * core
        arrived(wob.at[pl.ds(aligned(other * shard, shard), shard)], wo_recv.at[0, other, 0])

    far_owners = [(mirror, 0)] + far_others

    own_rows = wob.at[pl.ds(aligned(me * shard, shard), shard)]
    go(wo, own_rows, wo_tsend.at[0, 0, chips], wo_recv.at[0, me, 0], twin)
    for piece in range(heads):
        owner_loop(True, piece, piece + 1)
        wo_own_sends(piece)

    def mod(which):
        return jnp.where(half == 0, mods[which, 0:1, :], mods[which, 1:2, :])

    tall = min(128, span)
    blocks = packed // tall

    def start_step(step, carry):
        src = pl.ds(aligned(lax.rem(step, blocks) * tall, tall), tall)
        blk[pl.ds(aligned(step * tall, tall), tall), :] = jnp.dot(
            lat[src, :], w_two[lax.div(step, blocks)], preferred_element_type=jnp.float32
        )
        return carry

    lax.fori_loop(0, 2 * blocks, start_step, 0)

    @pl.when(is_spatial)
    def _():
        for slot in range(ROLES):
            arrived(latbuf.at[pl.ds(slot * packed, packed)], lat_recv.at[slot])

    @pl.when(jnp.logical_not(is_spatial))
    def _():
        for frame in range(n2):
            arrived(latbuf.at[pl.ds(frame * span, span)], lat_recv.at[frame])

    odd_span = lax.div(spot * span, packed)

    def hidden_step(step, carry):
        at = pl.ds(aligned(step * tall, tall), tall)
        frame, inner = lax.div(step, 2 * blocks), lax.rem(step, 2 * blocks)
        from_block = jnp.where(is_spatial, frame * blocks + lax.rem(inner, blocks), step)
        odd = jnp.where(is_spatial, lax.div(inner, blocks), odd_span)
        src = pl.ds(aligned(from_block * tall, tall), tall)
        begun = jnp.dot(latbuf[src, :], w_two[odd], preferred_element_type=jnp.float32)
        hbuf[at, :] = (normalize(begun) * (1.0 + mod(1)) + mod(0)).astype(jnp.bfloat16)
        return carry

    lax.fori_loop(0, rows // tall, hidden_step, 0)
    own_text.wait()

    def relay(head, part, off, over):
        view, number = slot_view(head, part, off), slot_sem(head, part, off)
        arrived(view, w_recv.at[number])
        if over:
            remote(view, view, w_xsend.at[number], w_recv.at[number], across).start()
        remote(view, view, w_tsend.at[number], w_recv.at[number], twin).start()

    groups = [(part, e) for part in range(3) for e in range(offs // 4)]

    def take_crossing(head):
        for part, e in groups:
            off = core + 2 * plane + 4 * e

            @pl.when(crosses(head, part, off))
            def _(part=part, off=off):
                relay(head, part, off, True)

    def take_near(head):
        for part, e in groups:
            off = core + 2 * plane + 4 * e

            @pl.when(jnp.logical_not(crosses(head, part, off)))
            def _(part=part, off=off):
                relay(head, part, off, False)

    def take_rest(head):
        for part, e in groups:
            relay(head, part, core + 2 * (1 - plane) + 4 * e, False)

    def take_twin(head):
        for part, e in groups:
            for side in range(2):
                off = 1 - core + 2 * side + 4 * e
                arrived(slot_view(head, part, off), w_recv.at[slot_sem(head, part, off)])

    def relay_end():
        for head in range(heads):
            for part, e in groups:
                off = core + 2 * plane + 4 * e
                view, number = slot_view(head, part, off), slot_sem(head, part, off)

                @pl.when(crosses(head, part, off))
                def _(view=view, number=number):
                    remote(view, view, w_xsend.at[number], w_recv.at[number], across).wait_send()

                for off in (core + 2 * plane + 4 * e, core + 2 * (1 - plane) + 4 * e):
                    view, number = slot_view(head, part, off), slot_sem(head, part, off)
                    remote(view, view, w_tsend.at[number], w_recv.at[number], twin).wait_send()

    finish.append(relay_end)

    words = tbuf.shape[0]

    def project(head, between=None):
        def body(turn, carry):
            at = pl.ds(aligned(turn * positions, positions), positions)
            pbuf[head, at, :] = dot_nt(hbuf[at, :], wbuf[head]).astype(jnp.bfloat16)
            return carry

        if between is None:
            lax.fori_loop(0, ROLES, body, 0)
        else:
            lax.fori_loop(0, ROLES // 2, body, 0)
            between()
            lax.fori_loop(ROLES // 2, ROLES, body, 0)

        @pl.when(is_spatial)
        def _():
            pbuf[head, pl.ds(rows, words), :] = dot_nt(tbuf[...], wbuf[head]).astype(jnp.bfloat16)

    scale = HDIM ** (-0.5)
    query_at, keys_at, vals_at = (pl.ds(part * HDIM, HDIM) for part in range(3))

    def lanes(head):
        return pl.ds(aligned((role * heads + head) * HDIM, HDIM), HDIM)

    def spatial_send(head, frame):
        to = half * n2 + spot * ROLES + frame
        src = obuf.at[head, pl.ds(aligned(frame * positions, positions), positions)]
        return (src, jbuf.at[:, lanes(head)], j_send.at[head, frame], j_recv.at[head, role]), to

    def temporal_send(head, frame):
        to = half * n2 + frame
        src = obuf.at[head, pl.ds(aligned(frame * span, span), span)]
        dst = jbuf.at[pl.ds(aligned(spot * span, span), span), lanes(head)]
        recv = j_recv.at[head, SROLES + (role - SROLES) * members + spot]
        return (src, dst, j_send.at[head, frame], recv), to

    def dispatch(refs, to):
        src, dst, send, recv = refs

        @pl.when(to == me)
        def _():
            pltpu.make_async_copy(src, dst, recv).start()

        @pl.when(to != me)
        def _():
            remote(src, dst, send, recv, {"seq": to}).start()

    def drain(refs, to):
        @pl.when(to != me)
        def _():
            remote(*refs, {"seq": to}).wait_send()

    def attend_spatial(head):
        live = jnp.where(half == 0, mask[0:1, :], mask[1:2, :]) > 0
        tallq = positions // 2

        def frame_step(frame, carry):
            base = frame * positions
            at = pl.ds(aligned(base, positions), positions)
            keys, vals = pbuf[head, at, keys_at], pbuf[head, at, vals_at]
            tkeys, tvals = pbuf[head, pl.ds(rows, words), keys_at], pbuf[head, pl.ds(rows, words), vals_at]
            for piece in range(2):
                here = pl.ds(aligned(base + piece * tallq, tallq), tallq)
                query = pbuf[head, here, query_at]
                near = dot_nt(query, keys) * scale
                side = jnp.where(live, dot_nt(query, tkeys) * scale, -1e30)
                top = jnp.maximum(
                    jnp.max(near, axis=-1, keepdims=True), jnp.max(side, axis=-1, keepdims=True)
                )
                near = jnp.exp(near - top)
                side = jnp.exp(side - top)
                total = jnp.sum(near, axis=-1, keepdims=True) + jnp.sum(side, axis=-1, keepdims=True)
                mixed = jnp.dot(
                    near.astype(jnp.bfloat16), vals, preferred_element_type=jnp.float32
                ) + jnp.dot(side.astype(jnp.bfloat16), tvals, preferred_element_type=jnp.float32)
                obuf[head, here, :] = (mixed / total).astype(jnp.bfloat16)
            dispatch(*spatial_send(head, frame))
            return carry

        lax.fori_loop(0, ROLES, frame_step, 0)

    def attend_temporal(head):
        few = 256 // n2
        size = few * n2
        row_at = lax.rem(lax.broadcasted_iota(jnp.int32, (size, size), 0), few)
        col_at = lax.rem(lax.broadcasted_iota(jnp.int32, (size, size), 1), few)
        same = row_at == col_at

        def place_step(place, carry):
            def at(frame):
                return pl.ds(aligned(frame * span + place * few, few), few)

            query, keys, vals = (
                jnp.concatenate([pbuf[head, at(frame), cols] for frame in range(n2)], axis=0)
                for cols in (query_at, keys_at, vals_at)
            )
            scores = jnp.where(same, dot_nt(query, keys) * scale, -1e30)
            weights = jnp.exp(scores - jnp.max(scores, axis=-1, keepdims=True))
            total = jnp.sum(weights, axis=-1, keepdims=True)
            mixed = jnp.dot(weights.astype(jnp.bfloat16), vals, preferred_element_type=jnp.float32)
            mixed = (mixed / total).astype(jnp.bfloat16)
            for frame in range(n2):
                obuf[head, at(frame), :] = mixed[frame * few : (frame + 1) * few]
            return carry

        lax.fori_loop(0, span // few, place_step, 0)

        def send_step(frame, carry):
            dispatch(*temporal_send(head, frame))
            return carry

        lax.fori_loop(0, n2, send_step, 0)

    def attend(head):
        @pl.when(is_spatial)
        def _():
            attend_spatial(head)

        @pl.when(jnp.logical_not(is_spatial))
        def _():
            attend_temporal(head)

    take_crossing(0)
    take_near(0)
    take_rest(0)
    take_twin(0)
    project(0, lambda: take_crossing(1))
    wo_near_take(0)
    wo_mirror(0)
    attend(0)
    take_near(1)
    take_crossing(2)
    take_rest(1)
    take_twin(1)
    project(1, lambda: wo_far_take(0))
    wo_near_take(1)
    wo_mirror(1)
    attend(1)
    wo_cross_take(0, others + far_owners)
    take_near(2)
    take_rest(2)
    take_twin(2)
    wo_mirror(2)
    project(2, lambda: wo_far_take(1))
    attend(2)
    wo_near_take(2)
    wo_cross_take(1, others)
    wo_own_wait()
    wo_wait(others)

    acc[...] = jnp.zeros_like(acc)
    strip = depth // 6

    for head in range(heads):
        for which in range(SROLES):
            lane = pl.ds((which * heads + head) * HDIM, HDIM)
            arrived(jbuf.at[:, lane], j_recv.at[head, which])
        for which in range(SROLES, ROLES):
            lane = pl.ds((which * heads + head) * HDIM, HDIM)
            for at in range(members):
                arrived(
                    jbuf.at[pl.ds(at * span, span), lane],
                    j_recv.at[head, SROLES + (which - SROLES) * members + at],
                )

    def mix_step(step, carry):
        cols = pl.ds(aligned(step * strip, strip), strip)
        gate = jnp.where(half == 0, mods[2, 0:1, cols], mods[2, 1:2, cols])
        value = blk[:, cols] + gate * dot_nt(jbuf[...], wob[cols, :])
        blk[:, cols] = value
        part = value[:, :128]
        for piece in range(1, strip // 128):
            part = part + value[:, piece * 128 : (piece + 1) * 128]
        acc[...] += part
        return carry

    lax.fori_loop(3 * half, 3 * half + 3, mix_step, 0)
    wo_far_take(2)
    wo_cross_take(1, far_owners)
    wo_wait(far_owners)
    lax.fori_loop(3 - 3 * half, 6 - 3 * half, mix_step, 0)

    steps = 4
    low = packed // steps

    def swap(step):
        at = pl.ds(aligned(step * low, low), low)
        return remote(
            predb.at[0, at], predb.at[1, at], p_send.at[step], p_recv.at[step], {"seq": mirror}
        )

    def last_step(step, carry):
        pred = None
        for odd in range(2):
            at = pl.ds(aligned(odd * packed + step * low, low), low)
            mean = jnp.sum(acc[at, :], axis=-1, keepdims=True) / depth
            center = blk[at, :] - mean
            spread = jnp.mean(center * center, axis=-1, keepdims=True)
            final = center * lax.rsqrt(spread + EPS) * (1.0 + mod(4)) + mod(3)
            here = dot_nt(final.astype(jnp.bfloat16), wf_two[odd])
            pred = here if pred is None else pred + here
        predb[0, pl.ds(aligned(step * low, low), low), :] = pred.astype(jnp.bfloat16)
        swap(step).start()
        return carry

    lax.fori_loop(0, steps, last_step, 0)

    def guide_step(step, carry):
        at = pl.ds(aligned(step * low, low), low)
        swap(step).wait_recv()
        own = predb[0, at, :].astype(jnp.float32)
        other = predb[1, at, :].astype(jnp.float32)
        cond = jnp.where(half == 0, own, other)
        uncond = jnp.where(half == 0, other, own)
        out[at, :] = uncond + GUIDE * (cond - uncond)
        return carry

    lax.fori_loop(0, steps, guide_step, 0)

    def swap_end(step, carry):
        swap(step).wait_send()
        return carry

    lax.fori_loop(0, steps, swap_end, 0)

    for head in range(heads):

        @pl.when(is_spatial)
        def _(head=head):
            def end(frame, carry):
                drain(*spatial_send(head, frame))
                return carry

            lax.fori_loop(0, ROLES, end, 0)

        @pl.when(jnp.logical_not(is_spatial))
        def _(head=head):
            def end(frame, carry):
                drain(*temporal_send(head, frame))
                return carry

            lax.fori_loop(0, n2, end, 0)

    for end in finish:
        end()


def per_device(latent, text_embed, text_mask, modulation, w_in, w_qkv, w_attn_out, w_final):
    count = lax.axis_size("seq")
    positions = latent.shape[1] // CHAN
    depth = w_in.shape[1]
    n2 = count // 2
    members = n2 // ROLES
    width = HEADS * HDIM // ROLES
    cols = w_qkv.shape[1]
    gran = next(g for g in range(HDIM // 4, 0, -16) if cols % g == 0 and HDIM % (4 * g) == 0)
    heads = width // HDIM
    offs, mine = HDIM // gran, cols // gran
    chips = n2 // 2
    rows = ROLES * positions
    words = text_embed.shape[1]
    bf16, f32 = jnp.bfloat16, jnp.float32
    vmem, anywhere = pl.BlockSpec(memory_space=pltpu.VMEM), pl.BlockSpec(memory_space=pl.ANY)
    sem = pltpu.SemaphoreType.DMA
    guided = pl.pallas_call(
        functools.partial(block_kernel, count, gran),
        out_shape=jax.ShapeDtypeStruct((positions // 2, 2 * CHAN), f32),
        in_specs=[vmem, anywhere, vmem, vmem, vmem, anywhere, anywhere, vmem],
        out_specs=vmem,
        scratch_shapes=[
            pltpu.VMEM((rows, 2 * CHAN), bf16),
            pltpu.VMEM((2, 2 * CHAN, depth), bf16),
            pltpu.VMEM((2, 2 * CHAN, depth), bf16),
            pltpu.VMEM((3, width, depth), bf16),
            pltpu.VMEM((rows, depth), bf16),
            pltpu.VMEM((words, depth), bf16),
            pltpu.VMEM((3, rows + words, width), bf16),
            pltpu.VMEM((heads, rows, HDIM), bf16),
            pltpu.VMEM((depth, HEADS * HDIM), bf16),
            pltpu.VMEM((positions, HEADS * HDIM), bf16),
            pltpu.VMEM((positions, depth), f32),
            pltpu.VMEM((positions, 128), f32),
            pltpu.VMEM((2, positions // 2, 2 * CHAN), bf16),
            sem((SROLES + (ROLES - SROLES) * members,)),
            sem((max(n2, ROLES),)),
            sem((mine, 2, members // 2)),
            sem((heads * 3 * offs,)),
            sem((heads * 3 * offs,)),
            sem((heads * 3 * offs,)),
            sem((heads, 2, chips)),
            sem((heads, 2 * chips)),
            sem((heads, 2, 2 * chips)),
            sem((heads, count, 2)),
            sem((heads, max(n2, ROLES))),
            sem((heads, SROLES + (ROLES - SROLES) * members)),
            sem((4,)),
            sem((4,)),
            sem((2,)),
        ],
        compiler_params=pltpu.CompilerParams(
            collective_id=0, has_side_effects=True, vmem_limit_bytes=64000 * 1024
        ),
        name="block",
    )(
        latent.reshape(positions // 2, 2 * CHAN), text_embed, text_mask, jnp.transpose(modulation, (1, 0, 2)),
        w_in, w_qkv.T, w_attn_out.T, w_final.T,
    )
    return guided.reshape(1, positions * CHAN)


def solution(mesh):
    in_specs = (
        P(("groups", "seq"), None),
        P("groups", None, None),
        P("groups", None),
        P("groups", None, None),
        P(),
        P(None, "seq"),
        P(None, "seq"),
        P(),
    )
    out_specs = P(("groups", "seq"), None)
    return jax.shard_map(
        per_device, mesh=mesh, in_specs=in_specs, out_specs=out_specs, check_vma=False
    )
```

```python
import functools

import jax
import jax.numpy as jnp
from jax import lax
from jax.experimental import pallas as pl
from jax.experimental.pallas import tpu as pltpu
from jax.sharding import PartitionSpec as P

HDIM = 128
SHEADS = 6
THEADS = 6
CHAN = 64
HEADS = 12
ROLES = 4
SROLES = 2
ROLE_OF = ((0, 2, 3, 1), (2, 0, 1, 3))

EPS = 1e-06
GUIDE = 5.0
NT = (((1,), (1,)), ((), ()))


def pick(table, *at):
    if not at:
        return jnp.int32(table)
    picked = pick(table[0], *at[1:])
    for number in range(1, len(table)):
        picked = jnp.where(at[0] == number, pick(table[number], *at[1:]), picked)
    return picked


def dot_nt(a, b):
    return lax.dot_general(a, b, NT, preferred_element_type=jnp.float32)


def normalize(values):
    center = values - jnp.mean(values, axis=-1, keepdims=True)
    spread = jnp.mean(center * center, axis=-1, keepdims=True)
    return center * lax.rsqrt(spread + EPS)


def block_kernel(
    count, gran, lat, text, mask, mods, w_in, wq, wo, wf, out,
    latbuf, w_two, wf_two, wbuf, hbuf, tbuf, pbuf, obuf, wob, jbuf, blk, acc, predb,
    lat_send, lat_recv, w_send, w_xsend, w_tsend, w_recv, wo_send, wo_xsend, wo_tsend, wo_recv,
    j_send, j_recv, p_send, p_recv, loc,
):
    packed = lat.shape[0]
    positions = 2 * packed
    depth = w_in.shape[1]
    n2 = count // 2
    chips = n2 // 2
    team, me = lax.axis_index("groups"), lax.axis_index("seq")
    plane = lax.rem(team, 2)
    half = lax.div(me, n2)
    local = lax.rem(me, n2)
    core = lax.rem(me, 2)
    chip = lax.div(local, 2)
    role = pick(ROLE_OF, half, lax.rem(chip, ROLES))
    seat_of = [[row.index(which) for which in range(ROLES)] for row in ROLE_OF]
    members = n2 // ROLES
    pairs = members // 2
    spot = lax.div(chip, ROLES) * 2 + core
    span = positions // members
    rows = ROLES * positions
    width = wbuf.shape[1]
    heads = width // HDIM
    offs = HDIM // gran
    mine = wq.shape[0] // gran
    is_spatial = role < SROLES

    twin = {"seq": me + 1 - 2 * core}
    across = {"groups": team + 1 - 2 * plane}

    def device(side, which, at):
        return side * n2 + (lax.div(at, 2) * ROLES + pick(seat_of, side, which)) * 2 + lax.rem(at, 2)

    def remote(src, dst, send, recv, peer):
        return pltpu.make_async_remote_copy(
            src_ref=src, dst_ref=dst, send_sem=send, recv_sem=recv,
            device_id=peer, device_id_type=pl.DeviceIdType.MESH,
        )

    finish = []

    def go(src, dst, send, recv, peer):
        remote(src, dst, send, recv, peer).start()
        finish.append(lambda: remote(src, dst, send, recv, peer).wait_send())

    def push(src, dst, send, recv, to):
        def far():
            return remote(src, dst, send, recv, {"seq": to})

        @pl.when(to == me)
        def _():
            pltpu.make_async_copy(src, dst, recv).start()

        @pl.when(to != me)
        def _():
            far().start()

        def end():
            @pl.when(to != me)
            def _():
                far().wait_send()

        finish.append(end)

    def arrived(view, sem):
        pltpu.make_async_copy(view, view, sem).wait()

    def aligned(value, unit):
        return pl.multiple_of(value, unit)

    barrier = pltpu.get_barrier_semaphore()

    def greet(step, carry):
        peer = lax.rem(me + step, count)
        pl.semaphore_signal(barrier, inc=1, device_id={"seq": peer}, device_id_type=pl.DeviceIdType.MESH)
        return carry

    pl.semaphore_signal(barrier, inc=1, device_id=across, device_id_type=pl.DeviceIdType.MESH)
    lax.fori_loop(1, count, greet, 0)

    shard = wo.shape[0]
    unit = shard // (2 * heads)
    own_wo = pltpu.make_async_copy(wo, wob.at[pl.ds(aligned(me * shard, shard), shard)], loc.at[0])
    own_text = pltpu.make_async_copy(text.at[half], tbuf, loc.at[1])
    own_wo.start()
    own_text.start()
    chan = w_in.shape[0]
    none = jnp.zeros((chan, depth), jnp.bfloat16)
    for odd in range(2):
        for two, one in ((w_two, w_in), (wf_two, wf)):
            two[odd, pl.ds(odd * chan, chan), :] = one[...]
            two[odd, pl.ds((1 - odd) * chan, chan), :] = none
    pl.semaphore_wait(barrier, count)

    for which in range(SROLES):
        to = device(half, which, lax.div(local, ROLES))
        slot = lax.rem(local, ROLES)
        push(
            lat, latbuf.at[pl.ds(aligned(slot * packed, packed), packed)],
            lat_send.at[which], lat_recv.at[slot], to,
        )
    for which in range(SROLES, ROLES):
        for at in range(members):
            push(
                lat.at[pl.ds(at * span % packed, span)], latbuf.at[pl.ds(aligned(local * span, span), span)],
                lat_send.at[SROLES + (which - SROLES) * members + at], lat_recv.at[local],
                device(half, which, jnp.int32(at)),
            )

    def slot_view(head, part, off):
        return wbuf.at[head, pl.ds(aligned(part * HDIM + off * gran, gran), gran)]

    def slot_sem(head, part, off):
        return (head * 3 + part) * offs + off

    def crosses(head, part, off):
        column = (part * HEADS + role * heads + head) * HDIM + off * gran
        return lax.div(column, 2 * wq.shape[0]) != lax.div(me, 2)

    def owner_loop(begin, head_first, head_last):
        def visit(turn, carry):
            wanted, k = lax.div(turn, mine), lax.rem(turn, mine)
            number = me * mine + k
            off = lax.rem(number, offs)
            whole = lax.div(number, offs)
            part, head_at = lax.div(whole, HEADS), lax.rem(whole, HEADS)
            which, head = lax.div(head_at, heads), lax.rem(head_at, heads)
            src = wq.at[pl.ds(aligned(k * gran, gran), gran)]
            dst, recv = slot_view(head, part, off), w_recv.at[slot_sem(head, part, off)]
            turned = lax.rem(lax.div(off, 2), 2) == plane
            for far in (1, 0):
                side = half + far * (1 - 2 * half)
                for pair in range(pairs):
                    to = device(side, which, pair * 2 + lax.rem(off, 2))
                    stays = lax.div(to, 2) == lax.div(me, 2)
                    use = jnp.logical_and(head == wanted, jnp.logical_or(turned, stays))

                    @pl.when(jnp.logical_and(use, to != me))
                    def _(to=to, far=far, pair=pair):
                        copy = remote(src, dst, w_send.at[k, far, pair], recv, {"seq": to})
                        copy.start() if begin else copy.wait_send()

                    if begin and not far:

                        @pl.when(jnp.logical_and(use, to == me))
                        def _():
                            pltpu.make_async_copy(src, dst, recv).start()

            return carry

        lax.fori_loop(head_first * mine, head_last * mine, visit, 0)

    finish.append(lambda: owner_loop(False, 0, heads))

    def wo_view(owner, side, piece):
        if piece == heads - 1:
            return wob.at[pl.ds(aligned(owner * shard + 2 * piece * unit, unit), 2 * unit)]
        return wob.at[pl.ds(aligned(owner * shard + (2 * piece + side) * unit, unit), unit)]

    mirror = me + n2 * (1 - 2 * half)

    def in_half(step):
        return half * n2 + lax.rem(chip + step, chips) * 2 + core

    def in_other(step):
        return (1 - half) * n2 + lax.rem(chip + step, chips) * 2 + core

    def wo_own_sends(piece):
        if piece == heads - 1:
            src = wo.at[pl.ds(2 * piece * unit, 2 * unit)]
        else:
            src = wo.at[pl.ds(aligned((2 * piece + plane) * unit, unit), unit)]
        dst, recv = wo_view(me, plane, piece), wo_recv.at[piece, me, 0]
        go(src, dst, wo_send.at[piece, 0, 0], recv, {"seq": mirror})
        for step in range(1, chips):
            go(src, dst, wo_send.at[piece, 0, step], recv, {"seq": in_half(step)})

    def wo_spread(owner, number, piece):
        view = wo_view(owner, plane, piece)
        if piece < heads - 1:
            go(view, view, wo_xsend.at[piece, number], wo_recv.at[piece, owner, 1], across)
        go(view, view, wo_tsend.at[piece, 0, number], wo_recv.at[piece, owner, 0], twin)

    def wo_take(owner, number, piece):
        arrived(wo_view(owner, plane, piece), wo_recv.at[piece, owner, 0])
        wo_spread(owner, number, piece)

    others = [(in_half(step), step) for step in range(1, chips)]
    far_others = [(in_other(step), chips + step) for step in range(1, chips)]

    def wo_near_take(piece):
        for owner, number in others:
            wo_take(owner, number, piece)

    def wo_mirror(piece):
        view = wo_view(mirror, plane, piece)
        arrived(view, wo_recv.at[piece, mirror, 0])
        for step in range(1, chips):
            go(
                view, view, wo_send.at[piece, 1, step], wo_recv.at[piece, mirror, 0],
                {"seq": in_half(step)},
            )
        wo_spread(mirror, 0, piece)

    def wo_far_take(piece):
        for owner, number in far_others:
            wo_take(owner, number, piece)

    def wo_cross_take(piece, owners):
        for owner, number in owners:
            view = wo_view(owner, 1 - plane, piece)
            arrived(view, wo_recv.at[piece, owner, 1])
            go(view, view, wo_tsend.at[piece, 1, number], wo_recv.at[piece, owner, 1], twin)

    def wo_wait(owners):
        for piece in range(heads):
            for owner, _ in owners:
                owner = owner + 1 - 2 * core
                arrived(wo_view(owner, plane, piece), wo_recv.at[piece, owner, 0])
                if piece < heads - 1:
                    arrived(wo_view(owner, 1 - plane, piece), wo_recv.at[piece, owner, 1])

    def wo_own_wait():
        own_wo.wait()
        other = me + 1 - 2 * core
        arrived(wob.at[pl.ds(aligned(other * shard, shard), shard)], wo_recv.at[0, other, 0])

    far_owners = [(mirror, 0)] + far_others

    own_rows = wob.at[pl.ds(aligned(me * shard, shard), shard)]
    go(wo, own_rows, wo_tsend.at[0, 0, chips], wo_recv.at[0, me, 0], twin)
    for piece in range(heads):
        owner_loop(True, piece, piece + 1)
        wo_own_sends(piece)

    def mod(which):
        return jnp.where(half == 0, mods[which, 0:1, :], mods[which, 1:2, :])

    tall = min(128, span)
    blocks = packed // tall

    def start_step(step, carry):
        src = pl.ds(aligned(lax.rem(step, blocks) * tall, tall), tall)
        blk[pl.ds(aligned(step * tall, tall), tall), :] = jnp.dot(
            lat[src, :], w_two[lax.div(step, blocks)], preferred_element_type=jnp.float32
        )
        return carry

    lax.fori_loop(0, 2 * blocks, start_step, 0)

    @pl.when(is_spatial)
    def _():
        for slot in range(ROLES):
            arrived(latbuf.at[pl.ds(slot * packed, packed)], lat_recv.at[slot])

    @pl.when(jnp.logical_not(is_spatial))
    def _():
        for frame in range(n2):
            arrived(latbuf.at[pl.ds(frame * span, span)], lat_recv.at[frame])

    odd_span = lax.div(spot * span, packed)

    def hidden_step(step, carry):
        at = pl.ds(aligned(step * tall, tall), tall)
        frame, inner = lax.div(step, 2 * blocks), lax.rem(step, 2 * blocks)
        from_block = jnp.where(is_spatial, frame * blocks + lax.rem(inner, blocks), step)
        odd = jnp.where(is_spatial, lax.div(inner, blocks), odd_span)
        src = pl.ds(aligned(from_block * tall, tall), tall)
        begun = jnp.dot(latbuf[src, :], w_two[odd], preferred_element_type=jnp.float32)
        hbuf[at, :] = (normalize(begun) * (1.0 + mod(1)) + mod(0)).astype(jnp.bfloat16)
        return carry

    own_text.wait()

    def relay(head, part, off, over):
        view, number = slot_view(head, part, off), slot_sem(head, part, off)
        arrived(view, w_recv.at[number])
        if over:
            remote(view, view, w_xsend.at[number], w_recv.at[number], across).start()
        remote(view, view, w_tsend.at[number], w_recv.at[number], twin).start()

    groups = [(part, e) for part in range(3) for e in range(offs // 4)]

    def take_crossing(head):
        for part, e in groups:
            off = core + 2 * plane + 4 * e

            @pl.when(crosses(head, part, off))
            def _(part=part, off=off):
                relay(head, part, off, True)

    def take_near(head):
        for part, e in groups:
            off = core + 2 * plane + 4 * e

            @pl.when(jnp.logical_not(crosses(head, part, off)))
            def _(part=part, off=off):
                relay(head, part, off, False)

    def take_rest(head):
        for part, e in groups:
            relay(head, part, core + 2 * (1 - plane) + 4 * e, False)

    def take_twin(head):
        for part, e in groups:
            for side in range(2):
                off = 1 - core + 2 * side + 4 * e
                arrived(slot_view(head, part, off), w_recv.at[slot_sem(head, part, off)])

    def relay_end():
        for head in range(heads):
            for part, e in groups:
                off = core + 2 * plane + 4 * e
                view, number = slot_view(head, part, off), slot_sem(head, part, off)

                @pl.when(crosses(head, part, off))
                def _(view=view, number=number):
                    remote(view, view, w_xsend.at[number], w_recv.at[number], across).wait_send()

                for off in (core + 2 * plane + 4 * e, core + 2 * (1 - plane) + 4 * e):
                    view, number = slot_view(head, part, off), slot_sem(head, part, off)
                    remote(view, view, w_tsend.at[number], w_recv.at[number], twin).wait_send()

    finish.append(relay_end)

    words = tbuf.shape[0]

    def project(head, between=None):
        def body(turn, carry):
            at = pl.ds(aligned(turn * positions, positions), positions)
            pbuf[head, at, :] = dot_nt(hbuf[at, :], wbuf[head]).astype(jnp.bfloat16)
            return carry

        if between is None:
            lax.fori_loop(0, ROLES, body, 0)
        else:
            lax.fori_loop(0, ROLES // 2, body, 0)
            between()
            lax.fori_loop(ROLES // 2, ROLES, body, 0)

        @pl.when(is_spatial)
        def _():
            pbuf[head, pl.ds(rows, words), :] = dot_nt(tbuf[...], wbuf[head]).astype(jnp.bfloat16)

    scale = HDIM ** (-0.5)
    query_at, keys_at, vals_at = (pl.ds(part * HDIM, HDIM) for part in range(3))

    def lanes(head):
        return pl.ds(aligned((role * heads + head) * HDIM, HDIM), HDIM)

    def spatial_send(head, frame):
        to = half * n2 + spot * ROLES + frame
        src = obuf.at[head, pl.ds(aligned(frame * positions, positions), positions)]
        return (src, jbuf.at[:, lanes(head)], j_send.at[head, frame], j_recv.at[head, role]), to

    def temporal_send(head, frame):
        to = half * n2 + frame
        src = obuf.at[head, pl.ds(aligned(frame * span, span), span)]
        dst = jbuf.at[pl.ds(aligned(spot * span, span), span), lanes(head)]
        recv = j_recv.at[head, SROLES + (role - SROLES) * members + spot]
        return (src, dst, j_send.at[head, frame], recv), to

    def dispatch(refs, to):
        src, dst, send, recv = refs

        @pl.when(to == me)
        def _():
            pltpu.make_async_copy(src, dst, recv).start()

        @pl.when(to != me)
        def _():
            remote(src, dst, send, recv, {"seq": to}).start()

    def drain(refs, to):
        @pl.when(to != me)
        def _():
            remote(*refs, {"seq": to}).wait_send()

    def attend_spatial(head):
        live = jnp.where(half == 0, mask[0:1, :], mask[1:2, :]) > 0
        tallq = positions // 2

        def frame_step(frame, carry):
            base = frame * positions
            at = pl.ds(aligned(base, positions), positions)
            keys, vals = pbuf[head, at, keys_at], pbuf[head, at, vals_at]
            tkeys, tvals = pbuf[head, pl.ds(rows, words), keys_at], pbuf[head, pl.ds(rows, words), vals_at]
            for piece in range(2):
                here = pl.ds(aligned(base + piece * tallq, tallq), tallq)
                query = pbuf[head, here, query_at]
                near = dot_nt(query, keys) * scale
                side = jnp.where(live, dot_nt(query, tkeys) * scale, -1e30)
                top = jnp.maximum(
                    jnp.max(near, axis=-1, keepdims=True), jnp.max(side, axis=-1, keepdims=True)
                )
                near = jnp.exp(near - top)
                side = jnp.exp(side - top)
                total = jnp.sum(near, axis=-1, keepdims=True) + jnp.sum(side, axis=-1, keepdims=True)
                mixed = jnp.dot(
                    near.astype(jnp.bfloat16), vals, preferred_element_type=jnp.float32
                ) + jnp.dot(side.astype(jnp.bfloat16), tvals, preferred_element_type=jnp.float32)
                obuf[head, here, :] = (mixed / total).astype(jnp.bfloat16)
            dispatch(*spatial_send(head, frame))
            return carry

        lax.fori_loop(0, ROLES, frame_step, 0)

    def attend_temporal(head):
        few = 256 // n2
        size = few * n2
        row_at = lax.rem(lax.broadcasted_iota(jnp.int32, (size, size), 0), few)
        col_at = lax.rem(lax.broadcasted_iota(jnp.int32, (size, size), 1), few)
        same = row_at == col_at

        def place_step(place, carry):
            def at(frame):
                return pl.ds(aligned(frame * span + place * few, few), few)

            query, keys, vals = (
                jnp.concatenate([pbuf[head, at(frame), cols] for frame in range(n2)], axis=0)
                for cols in (query_at, keys_at, vals_at)
            )
            scores = jnp.where(same, dot_nt(query, keys) * scale, -1e30)
            weights = jnp.exp(scores - jnp.max(scores, axis=-1, keepdims=True))
            total = jnp.sum(weights, axis=-1, keepdims=True)
            mixed = jnp.dot(weights.astype(jnp.bfloat16), vals, preferred_element_type=jnp.float32)
            mixed = (mixed / total).astype(jnp.bfloat16)
            for frame in range(n2):
                obuf[head, at(frame), :] = mixed[frame * few : (frame + 1) * few]
            return carry

        lax.fori_loop(0, span // few, place_step, 0)

        def send_step(frame, carry):
            dispatch(*temporal_send(head, frame))
            return carry

        lax.fori_loop(0, n2, send_step, 0)

    def attend(head):
        @pl.when(is_spatial)
        def _():
            attend_spatial(head)

        @pl.when(jnp.logical_not(is_spatial))
        def _():
            attend_temporal(head)

    lax.fori_loop(0, 3 * (rows // tall) // 4, hidden_step, 0)
    take_crossing(0)
    lax.fori_loop(3 * (rows // tall) // 4, rows // tall, hidden_step, 0)
    take_near(0)
    take_rest(0)
    take_twin(0)
    project(0, lambda: take_crossing(1))
    wo_near_take(0)
    wo_mirror(0)
    attend(0)
    take_near(1)
    take_rest(1)
    take_twin(1)
    project(1, lambda: take_crossing(2))
    wo_far_take(0)
    wo_near_take(1)
    wo_mirror(1)
    attend(1)
    wo_cross_take(0, others + far_owners)
    take_near(2)
    take_rest(2)
    take_twin(2)
    wo_mirror(2)
    project(2, lambda: wo_far_take(1))
    attend(2)
    wo_near_take(2)
    wo_cross_take(1, others)
    wo_own_wait()
    wo_wait(others)

    acc[...] = jnp.zeros_like(acc)
    strip = depth // 6

    for head in range(heads):
        for which in range(SROLES):
            lane = pl.ds((which * heads + head) * HDIM, HDIM)
            arrived(jbuf.at[:, lane], j_recv.at[head, which])
        for which in range(SROLES, ROLES):
            lane = pl.ds((which * heads + head) * HDIM, HDIM)
            for at in range(members):
                arrived(
                    jbuf.at[pl.ds(at * span, span), lane],
                    j_recv.at[head, SROLES + (which - SROLES) * members + at],
                )

    def mix_step(step, carry):
        cols = pl.ds(aligned(step * strip, strip), strip)
        gate = jnp.where(half == 0, mods[2, 0:1, cols], mods[2, 1:2, cols])
        value = blk[:, cols] + gate * dot_nt(jbuf[...], wob[cols, :])
        blk[:, cols] = value
        part = value[:, :128]
        for piece in range(1, strip // 128):
            part = part + value[:, piece * 128 : (piece + 1) * 128]
        acc[...] += part
        return carry

    lax.fori_loop(3 * half, 3 * half + 3, mix_step, 0)
    wo_far_take(2)
    wo_cross_take(1, far_owners)
    wo_wait(far_owners)
    lax.fori_loop(3 - 3 * half, 6 - 3 * half, mix_step, 0)

    steps = 4
    low = packed // steps

    def swap(step):
        at = pl.ds(aligned(step * low, low), low)
        return remote(
            predb.at[0, at], predb.at[1, at], p_send.at[step], p_recv.at[step], {"seq": mirror}
        )

    def last_step(step, carry):
        pred = None
        for odd in range(2):
            at = pl.ds(aligned(odd * packed + step * low, low), low)
            mean = jnp.sum(acc[at, :], axis=-1, keepdims=True) / depth
            center = blk[at, :] - mean
            spread = jnp.mean(center * center, axis=-1, keepdims=True)
            final = center * lax.rsqrt(spread + EPS) * (1.0 + mod(4)) + mod(3)
            here = dot_nt(final.astype(jnp.bfloat16), wf_two[odd])
            pred = here if pred is None else pred + here
        predb[0, pl.ds(aligned(step * low, low), low), :] = pred.astype(jnp.bfloat16)
        swap(step).start()
        return carry

    lax.fori_loop(0, steps, last_step, 0)

    def guide_step(step, carry):
        at = pl.ds(aligned(step * low, low), low)
        swap(step).wait_recv()
        own = predb[0, at, :].astype(jnp.float32)
        other = predb[1, at, :].astype(jnp.float32)
        cond = jnp.where(half == 0, own, other)
        uncond = jnp.where(half == 0, other, own)
        out[at, :] = uncond + GUIDE * (cond - uncond)
        return carry

    lax.fori_loop(0, steps, guide_step, 0)

    def swap_end(step, carry):
        swap(step).wait_send()
        return carry

    lax.fori_loop(0, steps, swap_end, 0)

    for head in range(heads):

        @pl.when(is_spatial)
        def _(head=head):
            def end(frame, carry):
                drain(*spatial_send(head, frame))
                return carry

            lax.fori_loop(0, ROLES, end, 0)

        @pl.when(jnp.logical_not(is_spatial))
        def _(head=head):
            def end(frame, carry):
                drain(*temporal_send(head, frame))
                return carry

            lax.fori_loop(0, n2, end, 0)

    for end in finish:
        end()


def per_device(latent, text_embed, text_mask, modulation, w_in, w_qkv, w_attn_out, w_final):
    count = lax.axis_size("seq")
    positions = latent.shape[1] // CHAN
    depth = w_in.shape[1]
    n2 = count // 2
    members = n2 // ROLES
    width = HEADS * HDIM // ROLES
    cols = w_qkv.shape[1]
    gran = next(g for g in range(HDIM // 4, 0, -16) if cols % g == 0 and HDIM % (4 * g) == 0)
    heads = width // HDIM
    offs, mine = HDIM // gran, cols // gran
    chips = n2 // 2
    rows = ROLES * positions
    words = text_embed.shape[1]
    bf16, f32 = jnp.bfloat16, jnp.float32
    vmem, anywhere = pl.BlockSpec(memory_space=pltpu.VMEM), pl.BlockSpec(memory_space=pl.ANY)
    sem = pltpu.SemaphoreType.DMA
    guided = pl.pallas_call(
        functools.partial(block_kernel, count, gran),
        out_shape=jax.ShapeDtypeStruct((positions // 2, 2 * CHAN), f32),
        in_specs=[vmem, anywhere, vmem, vmem, vmem, anywhere, anywhere, vmem],
        out_specs=vmem,
        scratch_shapes=[
            pltpu.VMEM((rows, 2 * CHAN), bf16),
            pltpu.VMEM((2, 2 * CHAN, depth), bf16),
            pltpu.VMEM((2, 2 * CHAN, depth), bf16),
            pltpu.VMEM((3, width, depth), bf16),
            pltpu.VMEM((rows, depth), bf16),
            pltpu.VMEM((words, depth), bf16),
            pltpu.VMEM((3, rows + words, width), bf16),
            pltpu.VMEM((heads, rows, HDIM), bf16),
            pltpu.VMEM((depth, HEADS * HDIM), bf16),
            pltpu.VMEM((positions, HEADS * HDIM), bf16),
            pltpu.VMEM((positions, depth), f32),
            pltpu.VMEM((positions, 128), f32),
            pltpu.VMEM((2, positions // 2, 2 * CHAN), bf16),
            sem((SROLES + (ROLES - SROLES) * members,)),
            sem((max(n2, ROLES),)),
            sem((mine, 2, members // 2)),
            sem((heads * 3 * offs,)),
            sem((heads * 3 * offs,)),
            sem((heads * 3 * offs,)),
            sem((heads, 2, chips)),
            sem((heads, 2 * chips)),
            sem((heads, 2, 2 * chips)),
            sem((heads, count, 2)),
            sem((heads, max(n2, ROLES))),
            sem((heads, SROLES + (ROLES - SROLES) * members)),
            sem((4,)),
            sem((4,)),
            sem((2,)),
        ],
        compiler_params=pltpu.CompilerParams(
            collective_id=0, has_side_effects=True, vmem_limit_bytes=64000 * 1024
        ),
        name="block",
    )(
        latent.reshape(positions // 2, 2 * CHAN), text_embed, text_mask, jnp.transpose(modulation, (1, 0, 2)),
        w_in, w_qkv.T, w_attn_out.T, w_final.T,
    )
    return guided.reshape(1, positions * CHAN)


def solution(mesh):
    in_specs = (
        P(("groups", "seq"), None),
        P("groups", None, None),
        P("groups", None),
        P("groups", None, None),
        P(),
        P(None, "seq"),
        P(None, "seq"),
        P(),
    )
    out_specs = P(("groups", "seq"), None)
    return jax.shard_map(
        per_device, mesh=mesh, in_specs=in_specs, out_specs=out_specs, check_vma=False
    )
```

```python
import functools

import jax
import jax.numpy as jnp
from jax import lax
from jax.experimental import pallas as pl
from jax.experimental.pallas import tpu as pltpu
from jax.sharding import PartitionSpec as P

HDIM = 128
SHEADS = 6
THEADS = 6
CHAN = 64
HEADS = 12
ROLES = 4
SROLES = 2
ROLE_OF = ((0, 2, 3, 1), (2, 0, 1, 3))

EPS = 1e-06
GUIDE = 5.0
NT = (((1,), (1,)), ((), ()))


def pick(table, *at):
    if not at:
        return jnp.int32(table)
    picked = pick(table[0], *at[1:])
    for number in range(1, len(table)):
        picked = jnp.where(at[0] == number, pick(table[number], *at[1:]), picked)
    return picked


def dot_nt(a, b):
    return lax.dot_general(a, b, NT, preferred_element_type=jnp.float32)


def normalize(values):
    center = values - jnp.mean(values, axis=-1, keepdims=True)
    spread = jnp.mean(center * center, axis=-1, keepdims=True)
    return center * lax.rsqrt(spread + EPS)


def block_kernel(
    count, gran, lat, text, mask, mods, w_in, wq, wo, wf, out,
    latbuf, w_two, wf_two, wbuf, hbuf, tbuf, pbuf, obuf, wob, jbuf, blk, acc, predb,
    lat_send, lat_recv, w_send, w_xsend, w_tsend, w_recv, wo_send, wo_xsend, wo_tsend, wo_recv,
    j_send, j_recv, p_send, p_recv, loc,
):
    packed = lat.shape[0]
    positions = 2 * packed
    depth = w_in.shape[1]
    n2 = count // 2
    chips = n2 // 2
    team, me = lax.axis_index("groups"), lax.axis_index("seq")
    plane = lax.rem(team, 2)
    half = lax.div(me, n2)
    local = lax.rem(me, n2)
    core = lax.rem(me, 2)
    chip = lax.div(local, 2)
    role = pick(ROLE_OF, half, lax.rem(chip, ROLES))
    seat_of = [[row.index(which) for which in range(ROLES)] for row in ROLE_OF]
    members = n2 // ROLES
    pairs = members // 2
    spot = lax.div(chip, ROLES) * 2 + core
    span = positions // members
    rows = ROLES * positions
    width = wbuf.shape[1]
    heads = width // HDIM
    offs = HDIM // gran
    mine = wq.shape[0] // gran
    is_spatial = role < SROLES

    twin = {"seq": me + 1 - 2 * core}
    across = {"groups": team + 1 - 2 * plane}

    def device(side, which, at):
        return side * n2 + (lax.div(at, 2) * ROLES + pick(seat_of, side, which)) * 2 + lax.rem(at, 2)

    def remote(src, dst, send, recv, peer):
        return pltpu.make_async_remote_copy(
            src_ref=src, dst_ref=dst, send_sem=send, recv_sem=recv,
            device_id=peer, device_id_type=pl.DeviceIdType.MESH,
        )

    finish = []

    def go(src, dst, send, recv, peer):
        remote(src, dst, send, recv, peer).start()
        finish.append(lambda: remote(src, dst, send, recv, peer).wait_send())

    def push(src, dst, send, recv, to):
        def far():
            return remote(src, dst, send, recv, {"seq": to})

        @pl.when(to == me)
        def _():
            pltpu.make_async_copy(src, dst, recv).start()

        @pl.when(to != me)
        def _():
            far().start()

        def end():
            @pl.when(to != me)
            def _():
                far().wait_send()

        finish.append(end)

    def arrived(view, sem):
        pltpu.make_async_copy(view, view, sem).wait()

    def aligned(value, unit):
        return pl.multiple_of(value, unit)

    barrier = pltpu.get_barrier_semaphore()

    def greet(step, carry):
        peer = lax.rem(me + step, count)
        pl.semaphore_signal(barrier, inc=1, device_id={"seq": peer}, device_id_type=pl.DeviceIdType.MESH)
        return carry

    pl.semaphore_signal(barrier, inc=1, device_id=across, device_id_type=pl.DeviceIdType.MESH)
    lax.fori_loop(1, count, greet, 0)

    shard = wo.shape[0]
    unit = shard // (2 * heads)
    own_wo = pltpu.make_async_copy(wo, wob.at[pl.ds(aligned(me * shard, shard), shard)], loc.at[0])
    own_text = pltpu.make_async_copy(text.at[half], tbuf, loc.at[1])
    own_wo.start()
    own_text.start()
    chan = w_in.shape[0]
    none = jnp.zeros((chan, depth), jnp.bfloat16)
    for odd in range(2):
        for two, one in ((w_two, w_in), (wf_two, wf)):
            two[odd, pl.ds(odd * chan, chan), :] = one[...]
            two[odd, pl.ds((1 - odd) * chan, chan), :] = none
    pl.semaphore_wait(barrier, count)

    for which in range(SROLES):
        to = device(half, which, lax.div(local, ROLES))
        slot = lax.rem(local, ROLES)
        push(
            lat, latbuf.at[pl.ds(aligned(slot * packed, packed), packed)],
            lat_send.at[which], lat_recv.at[slot], to,
        )
    for which in range(SROLES, ROLES):
        for at in range(members):
            push(
                lat.at[pl.ds(at * span % packed, span)], latbuf.at[pl.ds(aligned(local * span, span), span)],
                lat_send.at[SROLES + (which - SROLES) * members + at], lat_recv.at[local],
                device(half, which, jnp.int32(at)),
            )

    def slot_view(head, part, off):
        return wbuf.at[head, pl.ds(aligned(part * HDIM + off * gran, gran), gran)]

    def slot_sem(head, part, off):
        return (head * 3 + part) * offs + off

    def crosses(head, part, off):
        column = (part * HEADS + role * heads + head) * HDIM + off * gran
        return lax.div(column, 2 * wq.shape[0]) != lax.div(me, 2)

    def owner_loop(begin, head_first, head_last):
        def visit(turn, carry):
            wanted, k = lax.div(turn, mine), lax.rem(turn, mine)
            number = me * mine + k
            off = lax.rem(number, offs)
            whole = lax.div(number, offs)
            part, head_at = lax.div(whole, HEADS), lax.rem(whole, HEADS)
            which, head = lax.div(head_at, heads), lax.rem(head_at, heads)
            src = wq.at[pl.ds(aligned(k * gran, gran), gran)]
            dst, recv = slot_view(head, part, off), w_recv.at[slot_sem(head, part, off)]
            turned = lax.rem(lax.div(off, 2), 2) == plane
            for far in (1, 0):
                side = half + far * (1 - 2 * half)
                for pair in range(pairs):
                    to = device(side, which, pair * 2 + lax.rem(off, 2))
                    stays = lax.div(to, 2) == lax.div(me, 2)
                    use = jnp.logical_and(head == wanted, jnp.logical_or(turned, stays))

                    @pl.when(jnp.logical_and(use, to != me))
                    def _(to=to, far=far, pair=pair):
                        copy = remote(src, dst, w_send.at[k, far, pair], recv, {"seq": to})
                        copy.start() if begin else copy.wait_send()

                    if begin and not far:

                        @pl.when(jnp.logical_and(use, to == me))
                        def _():
                            pltpu.make_async_copy(src, dst, recv).start()

            return carry

        lax.fori_loop(head_first * mine, head_last * mine, visit, 0)

    finish.append(lambda: owner_loop(False, 0, heads))

    def wo_view(owner, side, piece):
        if piece == heads - 1:
            return wob.at[pl.ds(aligned(owner * shard + 2 * piece * unit, unit), 2 * unit)]
        return wob.at[pl.ds(aligned(owner * shard + (2 * piece + side) * unit, unit), unit)]

    mirror = me + n2 * (1 - 2 * half)

    def in_half(step):
        return half * n2 + lax.rem(chip + step, chips) * 2 + core

    def in_other(step):
        return (1 - half) * n2 + lax.rem(chip + step, chips) * 2 + core

    def wo_own_sends(piece):
        if piece == heads - 1:
            src = wo.at[pl.ds(2 * piece * unit, 2 * unit)]
        else:
            src = wo.at[pl.ds(aligned((2 * piece + plane) * unit, unit), unit)]
        dst, recv = wo_view(me, plane, piece), wo_recv.at[piece, me, 0]
        go(src, dst, wo_send.at[piece, 0, 0], recv, {"seq": mirror})
        for step in range(1, chips):
            go(src, dst, wo_send.at[piece, 0, step], recv, {"seq": in_half(step)})

    def wo_spread(owner, number, piece):
        view = wo_view(owner, plane, piece)
        if piece < heads - 1:
            go(view, view, wo_xsend.at[piece, number], wo_recv.at[piece, owner, 1], across)
        go(view, view, wo_tsend.at[piece, 0, number], wo_recv.at[piece, owner, 0], twin)

    def wo_take(owner, number, piece):
        arrived(wo_view(owner, plane, piece), wo_recv.at[piece, owner, 0])
        wo_spread(owner, number, piece)

    others = [(in_half(step), step) for step in range(1, chips)]
    far_others = [(in_other(step), chips + step) for step in range(1, chips)]

    def wo_near_take(piece):
        for owner, number in others:
            wo_take(owner, number, piece)

    def wo_mirror(piece):
        view = wo_view(mirror, plane, piece)
        arrived(view, wo_recv.at[piece, mirror, 0])
        for step in range(1, chips):
            go(
                view, view, wo_send.at[piece, 1, step], wo_recv.at[piece, mirror, 0],
                {"seq": in_half(step)},
            )
        wo_spread(mirror, 0, piece)

    def wo_far_take(piece):
        for owner, number in far_others:
            wo_take(owner, number, piece)

    def wo_cross_take(piece, owners):
        for owner, number in owners:
            view = wo_view(owner, 1 - plane, piece)
            arrived(view, wo_recv.at[piece, owner, 1])
            go(view, view, wo_tsend.at[piece, 1, number], wo_recv.at[piece, owner, 1], twin)

    def wo_wait(owners):
        for piece in range(heads):
            for owner, _ in owners:
                owner = owner + 1 - 2 * core
                arrived(wo_view(owner, plane, piece), wo_recv.at[piece, owner, 0])
                if piece < heads - 1:
                    arrived(wo_view(owner, 1 - plane, piece), wo_recv.at[piece, owner, 1])

    def wo_own_wait():
        own_wo.wait()
        other = me + 1 - 2 * core
        arrived(wob.at[pl.ds(aligned(other * shard, shard), shard)], wo_recv.at[0, other, 0])

    far_owners = [(mirror, 0)] + far_others

    own_rows = wob.at[pl.ds(aligned(me * shard, shard), shard)]
    go(wo, own_rows, wo_tsend.at[0, 0, chips], wo_recv.at[0, me, 0], twin)
    for piece in range(heads):
        owner_loop(True, piece, piece + 1)
        wo_own_sends(piece)

    def mod(which):
        return jnp.where(half == 0, mods[which, 0:1, :], mods[which, 1:2, :])

    tall = min(128, span)
    blocks = packed // tall

    def start_step(step, carry):
        src = pl.ds(aligned(lax.rem(step, blocks) * tall, tall), tall)
        blk[pl.ds(aligned(step * tall, tall), tall), :] = jnp.dot(
            lat[src, :], w_two[lax.div(step, blocks)], preferred_element_type=jnp.float32
        )
        return carry

    lax.fori_loop(0, 2 * blocks, start_step, 0)

    @pl.when(is_spatial)
    def _():
        for slot in range(ROLES):
            arrived(latbuf.at[pl.ds(slot * packed, packed)], lat_recv.at[slot])

    @pl.when(jnp.logical_not(is_spatial))
    def _():
        for frame in range(n2):
            arrived(latbuf.at[pl.ds(frame * span, span)], lat_recv.at[frame])

    odd_span = lax.div(spot * span, packed)

    def hidden_step(step, carry):
        at = pl.ds(aligned(step * tall, tall), tall)
        frame, inner = lax.div(step, 2 * blocks), lax.rem(step, 2 * blocks)
        from_block = jnp.where(is_spatial, frame * blocks + lax.rem(inner, blocks), step)
        odd = jnp.where(is_spatial, lax.div(inner, blocks), odd_span)
        src = pl.ds(aligned(from_block * tall, tall), tall)
        begun = jnp.dot(latbuf[src, :], w_two[odd], preferred_element_type=jnp.float32)
        hbuf[at, :] = (normalize(begun) * (1.0 + mod(1)) + mod(0)).astype(jnp.bfloat16)
        return carry

    own_text.wait()

    def relay(head, part, off, over):
        view, number = slot_view(head, part, off), slot_sem(head, part, off)
        arrived(view, w_recv.at[number])
        if over:
            remote(view, view, w_xsend.at[number], w_recv.at[number], across).start()
        remote(view, view, w_tsend.at[number], w_recv.at[number], twin).start()

    groups = [(part, e) for part in range(3) for e in range(offs // 4)]

    def take_crossing(head):
        for part, e in groups:
            off = core + 2 * plane + 4 * e

            @pl.when(crosses(head, part, off))
            def _(part=part, off=off):
                relay(head, part, off, True)

    def take_near(head):
        for part, e in groups:
            off = core + 2 * plane + 4 * e

            @pl.when(jnp.logical_not(crosses(head, part, off)))
            def _(part=part, off=off):
                relay(head, part, off, False)

    def take_rest(head):
        for part, e in groups:
            relay(head, part, core + 2 * (1 - plane) + 4 * e, False)

    def take_twin(head):
        for part, e in groups:
            for side in range(2):
                off = 1 - core + 2 * side + 4 * e
                arrived(slot_view(head, part, off), w_recv.at[slot_sem(head, part, off)])

    def relay_end():
        for head in range(heads):
            for part, e in groups:
                off = core + 2 * plane + 4 * e
                view, number = slot_view(head, part, off), slot_sem(head, part, off)

                @pl.when(crosses(head, part, off))
                def _(view=view, number=number):
                    remote(view, view, w_xsend.at[number], w_recv.at[number], across).wait_send()

                for off in (core + 2 * plane + 4 * e, core + 2 * (1 - plane) + 4 * e):
                    view, number = slot_view(head, part, off), slot_sem(head, part, off)
                    remote(view, view, w_tsend.at[number], w_recv.at[number], twin).wait_send()

    finish.append(relay_end)

    words = tbuf.shape[0]

    def project(head, between=None):
        def body(turn, carry):
            at = pl.ds(aligned(turn * positions, positions), positions)
            pbuf[head, at, :] = dot_nt(hbuf[at, :], wbuf[head]).astype(jnp.bfloat16)
            return carry

        if between is None:
            lax.fori_loop(0, ROLES, body, 0)
        else:
            lax.fori_loop(0, ROLES // 2, body, 0)
            between()
            lax.fori_loop(ROLES // 2, ROLES, body, 0)

        @pl.when(is_spatial)
        def _():
            pbuf[head, pl.ds(rows, words), :] = dot_nt(tbuf[...], wbuf[head]).astype(jnp.bfloat16)

    scale = HDIM ** (-0.5)
    query_at, keys_at, vals_at = (pl.ds(part * HDIM, HDIM) for part in range(3))

    def lanes(head):
        return pl.ds(aligned((role * heads + head) * HDIM, HDIM), HDIM)

    def spatial_send(head, frame):
        to = half * n2 + spot * ROLES + frame
        src = obuf.at[head, pl.ds(aligned(frame * positions, positions), positions)]
        return (src, jbuf.at[:, lanes(head)], j_send.at[head, frame], j_recv.at[head, role]), to

    def temporal_send(head, frame):
        to = half * n2 + frame
        src = obuf.at[head, pl.ds(aligned(frame * span, span), span)]
        dst = jbuf.at[pl.ds(aligned(spot * span, span), span), lanes(head)]
        recv = j_recv.at[head, SROLES + (role - SROLES) * members + spot]
        return (src, dst, j_send.at[head, frame], recv), to

    def dispatch(refs, to):
        src, dst, send, recv = refs

        @pl.when(to == me)
        def _():
            pltpu.make_async_copy(src, dst, recv).start()

        @pl.when(to != me)
        def _():
            remote(src, dst, send, recv, {"seq": to}).start()

    def drain(refs, to):
        @pl.when(to != me)
        def _():
            remote(*refs, {"seq": to}).wait_send()

    def attend_spatial(head):
        live = jnp.where(half == 0, mask[0:1, :], mask[1:2, :]) > 0
        tallq = positions // 2

        def frame_step(frame, carry):
            base = frame * positions
            at = pl.ds(aligned(base, positions), positions)
            keys, vals = pbuf[head, at, keys_at], pbuf[head, at, vals_at]
            tkeys, tvals = pbuf[head, pl.ds(rows, words), keys_at], pbuf[head, pl.ds(rows, words), vals_at]
            for piece in range(2):
                here = pl.ds(aligned(base + piece * tallq, tallq), tallq)
                query = pbuf[head, here, query_at]
                near = dot_nt(query, keys) * scale
                side = jnp.where(live, dot_nt(query, tkeys) * scale, -1e30)
                top = jnp.maximum(
                    jnp.max(near, axis=-1, keepdims=True), jnp.max(side, axis=-1, keepdims=True)
                )
                near = jnp.exp(near - top)
                side = jnp.exp(side - top)
                total = jnp.sum(near, axis=-1, keepdims=True) + jnp.sum(side, axis=-1, keepdims=True)
                mixed = jnp.dot(
                    near.astype(jnp.bfloat16), vals, preferred_element_type=jnp.float32
                ) + jnp.dot(side.astype(jnp.bfloat16), tvals, preferred_element_type=jnp.float32)
                obuf[head, here, :] = (mixed / total).astype(jnp.bfloat16)
            dispatch(*spatial_send(head, frame))
            return carry

        lax.fori_loop(0, ROLES, frame_step, 0)

    def attend_temporal(head):
        few = 256 // n2
        size = few * n2
        row_at = lax.rem(lax.broadcasted_iota(jnp.int32, (size, size), 0), few)
        col_at = lax.rem(lax.broadcasted_iota(jnp.int32, (size, size), 1), few)
        same = row_at == col_at

        def place_step(place, carry):
            def at(frame):
                return pl.ds(aligned(frame * span + place * few, few), few)

            query, keys, vals = (
                jnp.concatenate([pbuf[head, at(frame), cols] for frame in range(n2)], axis=0)
                for cols in (query_at, keys_at, vals_at)
            )
            scores = jnp.where(same, dot_nt(query, keys) * scale, -1e30)
            weights = jnp.exp(scores - jnp.max(scores, axis=-1, keepdims=True))
            total = jnp.sum(weights, axis=-1, keepdims=True)
            mixed = jnp.dot(weights.astype(jnp.bfloat16), vals, preferred_element_type=jnp.float32)
            mixed = (mixed / total).astype(jnp.bfloat16)
            for frame in range(n2):
                obuf[head, at(frame), :] = mixed[frame * few : (frame + 1) * few]
            return carry

        lax.fori_loop(0, span // few, place_step, 0)

        def send_step(frame, carry):
            dispatch(*temporal_send(head, frame))
            return carry

        lax.fori_loop(0, n2, send_step, 0)

    def attend(head):
        @pl.when(is_spatial)
        def _():
            attend_spatial(head)

        @pl.when(jnp.logical_not(is_spatial))
        def _():
            attend_temporal(head)

    lax.fori_loop(0, 3 * (rows // tall) // 4, hidden_step, 0)
    take_crossing(0)
    lax.fori_loop(3 * (rows // tall) // 4, rows // tall, hidden_step, 0)
    take_near(0)
    take_rest(0)
    take_twin(0)
    project(0, lambda: take_crossing(1))
    wo_near_take(0)
    wo_mirror(0)
    attend(0)
    take_near(1)
    take_rest(1)
    take_twin(1)
    project(1, lambda: take_crossing(2))
    wo_near_take(1)
    wo_mirror(1)
    attend(1)
    wo_far_take(0)
    take_near(2)
    take_rest(2)
    take_twin(2)
    wo_mirror(2)
    project(2, lambda: wo_far_take(1))
    attend(2)
    wo_near_take(2)
    wo_cross_take(0, others + far_owners)
    wo_cross_take(1, others)
    wo_own_wait()
    wo_wait(others)

    acc[...] = jnp.zeros_like(acc)
    strip = depth // 6

    for head in range(heads):
        for which in range(SROLES):
            lane = pl.ds((which * heads + head) * HDIM, HDIM)
            arrived(jbuf.at[:, lane], j_recv.at[head, which])
        for which in range(SROLES, ROLES):
            lane = pl.ds((which * heads + head) * HDIM, HDIM)
            for at in range(members):
                arrived(
                    jbuf.at[pl.ds(at * span, span), lane],
                    j_recv.at[head, SROLES + (which - SROLES) * members + at],
                )

    def mix_step(step, carry):
        cols = pl.ds(aligned(step * strip, strip), strip)
        gate = jnp.where(half == 0, mods[2, 0:1, cols], mods[2, 1:2, cols])
        value = blk[:, cols] + gate * dot_nt(jbuf[...], wob[cols, :])
        blk[:, cols] = value
        part = value[:, :128]
        for piece in range(1, strip // 128):
            part = part + value[:, piece * 128 : (piece + 1) * 128]
        acc[...] += part
        return carry

    lax.fori_loop(3 * half, 3 * half + 3, mix_step, 0)
    wo_far_take(2)
    wo_cross_take(1, far_owners)
    wo_wait(far_owners)
    lax.fori_loop(3 - 3 * half, 6 - 3 * half, mix_step, 0)

    steps = 4
    low = packed // steps

    def swap(step):
        at = pl.ds(aligned(step * low, low), low)
        return remote(
            predb.at[0, at], predb.at[1, at], p_send.at[step], p_recv.at[step], {"seq": mirror}
        )

    def last_step(step, carry):
        pred = None
        for odd in range(2):
            at = pl.ds(aligned(odd * packed + step * low, low), low)
            mean = jnp.sum(acc[at, :], axis=-1, keepdims=True) / depth
            center = blk[at, :] - mean
            spread = jnp.mean(center * center, axis=-1, keepdims=True)
            final = center * lax.rsqrt(spread + EPS) * (1.0 + mod(4)) + mod(3)
            here = dot_nt(final.astype(jnp.bfloat16), wf_two[odd])
            pred = here if pred is None else pred + here
        predb[0, pl.ds(aligned(step * low, low), low), :] = pred.astype(jnp.bfloat16)
        swap(step).start()
        return carry

    lax.fori_loop(0, steps, last_step, 0)

    def guide_step(step, carry):
        at = pl.ds(aligned(step * low, low), low)
        swap(step).wait_recv()
        own = predb[0, at, :].astype(jnp.float32)
        other = predb[1, at, :].astype(jnp.float32)
        cond = jnp.where(half == 0, own, other)
        uncond = jnp.where(half == 0, other, own)
        out[at, :] = uncond + GUIDE * (cond - uncond)
        return carry

    lax.fori_loop(0, steps, guide_step, 0)

    def swap_end(step, carry):
        swap(step).wait_send()
        return carry

    lax.fori_loop(0, steps, swap_end, 0)

    for head in range(heads):

        @pl.when(is_spatial)
        def _(head=head):
            def end(frame, carry):
                drain(*spatial_send(head, frame))
                return carry

            lax.fori_loop(0, ROLES, end, 0)

        @pl.when(jnp.logical_not(is_spatial))
        def _(head=head):
            def end(frame, carry):
                drain(*temporal_send(head, frame))
                return carry

            lax.fori_loop(0, n2, end, 0)

    for end in finish:
        end()


def per_device(latent, text_embed, text_mask, modulation, w_in, w_qkv, w_attn_out, w_final):
    count = lax.axis_size("seq")
    positions = latent.shape[1] // CHAN
    depth = w_in.shape[1]
    n2 = count // 2
    members = n2 // ROLES
    width = HEADS * HDIM // ROLES
    cols = w_qkv.shape[1]
    gran = next(g for g in range(HDIM // 4, 0, -16) if cols % g == 0 and HDIM % (4 * g) == 0)
    heads = width // HDIM
    offs, mine = HDIM // gran, cols // gran
    chips = n2 // 2
    rows = ROLES * positions
    words = text_embed.shape[1]
    bf16, f32 = jnp.bfloat16, jnp.float32
    vmem, anywhere = pl.BlockSpec(memory_space=pltpu.VMEM), pl.BlockSpec(memory_space=pl.ANY)
    sem = pltpu.SemaphoreType.DMA
    guided = pl.pallas_call(
        functools.partial(block_kernel, count, gran),
        out_shape=jax.ShapeDtypeStruct((positions // 2, 2 * CHAN), f32),
        in_specs=[vmem, anywhere, vmem, vmem, vmem, anywhere, anywhere, vmem],
        out_specs=vmem,
        scratch_shapes=[
            pltpu.VMEM((rows, 2 * CHAN), bf16),
            pltpu.VMEM((2, 2 * CHAN, depth), bf16),
            pltpu.VMEM((2, 2 * CHAN, depth), bf16),
            pltpu.VMEM((3, width, depth), bf16),
            pltpu.VMEM((rows, depth), bf16),
            pltpu.VMEM((words, depth), bf16),
            pltpu.VMEM((3, rows + words, width), bf16),
            pltpu.VMEM((heads, rows, HDIM), bf16),
            pltpu.VMEM((depth, HEADS * HDIM), bf16),
            pltpu.VMEM((positions, HEADS * HDIM), bf16),
            pltpu.VMEM((positions, depth), f32),
            pltpu.VMEM((positions, 128), f32),
            pltpu.VMEM((2, positions // 2, 2 * CHAN), bf16),
            sem((SROLES + (ROLES - SROLES) * members,)),
            sem((max(n2, ROLES),)),
            sem((mine, 2, members // 2)),
            sem((heads * 3 * offs,)),
            sem((heads * 3 * offs,)),
            sem((heads * 3 * offs,)),
            sem((heads, 2, chips)),
            sem((heads, 2 * chips)),
            sem((heads, 2, 2 * chips)),
            sem((heads, count, 2)),
            sem((heads, max(n2, ROLES))),
            sem((heads, SROLES + (ROLES - SROLES) * members)),
            sem((4,)),
            sem((4,)),
            sem((2,)),
        ],
        compiler_params=pltpu.CompilerParams(
            collective_id=0, has_side_effects=True, vmem_limit_bytes=64000 * 1024
        ),
        name="block",
    )(
        latent.reshape(positions // 2, 2 * CHAN), text_embed, text_mask, jnp.transpose(modulation, (1, 0, 2)),
        w_in, w_qkv.T, w_attn_out.T, w_final.T,
    )
    return guided.reshape(1, positions * CHAN)


def solution(mesh):
    in_specs = (
        P(("groups", "seq"), None),
        P("groups", None, None),
        P("groups", None),
        P("groups", None, None),
        P(),
        P(None, "seq"),
        P(None, "seq"),
        P(),
    )
    out_specs = P(("groups", "seq"), None)
    return jax.shard_map(
        per_device, mesh=mesh, in_specs=in_specs, out_specs=out_specs, check_vma=False
    )
```
